32 devices in a mesh: lev: 4 (over x, core), sp: 8 (over z, y).
Axes of the slice: x: 2, y: 2, z: 4, core: 2. Of those that a mesh axis runs over, the one named last changes fastest.
Arguments:
- ocean_state: bfloat16 [32, 8, 128, 200], P(None, None, 'sp', 'lev'), may hold values from -18 to 18
- slot_level: int32 [20], replicated, may hold values from 0 to 19, each once
- wet_mask: int32 [32, 128], P('lev', 'sp'), may hold values 0 or 1
- w_in: bfloat16 [190, 800], replicated, may hold values from -0.4375 to 0.4375
- b_in: float32 [800], replicated, may hold values from -3 to 3
- w_depth: bfloat16 [7, 7, 800], replicated, may hold values from -0.875 to 0.875
- norm_gain: float32 [800], replicated, may hold values from 0.1 to 1.9
- norm_bias: float32 [800], replicated, may hold values from -3 to 3
- w_one: bfloat16 [800, 3200], replicated, may hold values from -0.21875 to 0.21875
- b_one: float32 [3200], replicated, may hold values from -3 to 3
- w_two: bfloat16 [3200, 800], replicated, may hold values from -0.109375 to 0.109375
- b_two: float32 [800], replicated, may hold values from -3 to 3
- w_out: bfloat16 [800, 190], replicated, may hold values from -0.21875 to 0.21875
- b_out: float32 [190], replicated, may hold values from -3 to 3
- cotangent: bfloat16 [32, 8, 128, 200], P(None, None, 'sp', 'lev'), may hold values from -6 to 6
Outputs:
- next_state: bfloat16 [32, 8, 128, 200], P(None, None, 'sp', 'lev')
- grad_ocean_state: bfloat16 [32, 8, 128, 200], P(None, None, 'sp', 'lev')
- grad_w_in: float32 [190, 800], replicated
- grad_b_in: float32 [800], replicated
- grad_w_depth: float32 [7, 7, 800], replicated
- grad_norm_gain: float32 [800], replicated
- grad_norm_bias: float32 [800], replicated
- grad_w_one: float32 [800, 3200], replicated
- grad_b_one: float32 [3200], replicated
- grad_w_two: float32 [3200, 800], replicated
- grad_b_two: float32 [800], replicated
- grad_w_out: float32 [800, 190], replicated
- grad_b_out: float32 [190], replicated
The draws below stay inside these ranges and needn't reach their ends.
Inputs may be any that keep to these rules, and one draw needn't show every extreme that they name: `slot_level`: each depth level 0 to 18 stands in exactly one level slot; values 19 or more mark empty slots. Slots g * 5 to (g + 1) * 5 - 1 form group g, whose channels are slot channels g * 50 to (g + 1) * 50 - 1.
All inputs are finite; a program needn't handle non-finite values. No bound on the sum of `wet_mask` on one device may be relied on, other than what follows from the above.
Results may differ from the reference program's by a relative error of at most 0.0076.
Values may be sent and summed in bfloat16 or wider, within the bound.
No kernel may reach another device: no remote copies, remote signals or barrier semaphores. Data moves between devices by JAX's collectives and lax.ppermute only.
A program may use at most 192 MiB of HBM per device.

```python
from functools import partial
import jax
import jax.numpy as jnp
from jax import lax

D = 800
FF = 3200
VARS = 10
KERNEL = 7
DATES = 8
LAT = 32
LON = 128
SLOTS = 20
SLOT_CHANNELS = 200
CHANNELS = 190


def draw_ocean_state(key, part):
    keys = jax.random.split(key, 3)
    lat_pos = jnp.arange(LAT).astype(jnp.float32) / LAT
    lon_pos = jnp.arange(LON).astype(jnp.float32) / LON
    lift = (1.0 + 2.0 * lat_pos)[:, None, None, None]
    rough = jax.random.uniform(keys[0], (LAT, 1, LON, 1), minval=0.7, maxval=1.4)
    phase = jax.random.uniform(keys[1], (1, 1, 1, SLOT_CHANNELS), minval=0.0, maxval=6.2831853)
    offset = 0.6 * jnp.sin(6.2831853 * lon_pos[None, None, :, None] + phase)
    shape = (LAT, DATES, LON, SLOT_CHANNELS)
    base = jnp.clip(jax.random.normal(keys[2], shape), -4.0, 4.0)
    return (offset + lift * rough * base).astype(jnp.bfloat16)


def touch_ends(values, rng, smallest, top_value):
    index_at = [jax.random.randint(jax.random.fold_in(rng, axis), (), 0, length) for axis, length in enumerate(values.shape)]
    widest = values.shape.index(max(values.shape))
    neighbour = index_at[:widest] + [(index_at[widest] + 1) % values.shape[widest]] + index_at[widest + 1:]
    return values.at[tuple(index_at)].set(smallest).at[tuple(neighbour)].set(top_value)


def block_levels(own_key, extent, pieces, smallest, high):
    level = 1.0
    for dim, blocks in pieces:
        draws = jax.random.uniform(jax.random.fold_in(jax.random.fold_in(own_key, 6), dim), (blocks,), jnp.float32, smallest / len(pieces), high / len(pieces))
        level = level * jnp.repeat(jnp.exp(draws), extent[dim] // blocks).reshape((-1,) + (1,) * (len(extent) - 1 - dim))
    return level


def bell_draw(rng, dims, deviation, limit, cuts=(), dtype=jnp.bfloat16):
    values = deviation * jax.random.normal(rng, dims, jnp.float32)
    if cuts:
        values = values * block_levels(rng, dims, cuts, -0.22, 0.18)
    return jnp.clip(values, -limit, limit).astype(dtype)


def setup_inputs(seed: int = 0) -> dict:
    seeds = jax.random.split(jax.random.key(seed), 16)
    return {
        "ocean_state": draw_ocean_state(jax.random.fold_in(seeds[15], 71), 0),
        "slot_level": jax.random.permutation(seeds[1], SLOTS).astype(jnp.int32),
        "wet_mask": touch_ends((jax.random.randint(seeds[2], (LAT, LON), 0, 10) < 7).astype(jnp.int32), jax.random.fold_in(seeds[2], 1), 0, 1),
        "w_in": bell_draw(seeds[3], (CHANNELS, D), CHANNELS ** -0.5, 0.4375),
        "b_in": bell_draw(seeds[4], (D,), 0.5, 3.0, (), jnp.float32),
        "w_depth": bell_draw(seeds[5], (KERNEL, KERNEL, D), (KERNEL * KERNEL) ** -0.5, 0.875),
        "norm_gain": jnp.clip(1.0 + 0.18 * jax.random.normal(seeds[6], (D,), jnp.float32), 0.1, 1.9),
        "norm_bias": bell_draw(seeds[7], (D,), 0.5, 3.0, (), jnp.float32),
        "w_one": bell_draw(seeds[8], (D, FF), D ** -0.5, 0.21875),
        "b_one": bell_draw(seeds[9], (FF,), 0.5, 3.0, (), jnp.float32),
        "w_two": bell_draw(seeds[10], (FF, D), FF ** -0.5, 0.109375),
        "b_two": bell_draw(seeds[11], (D,), 0.5, 3.0, (), jnp.float32),
        "w_out": bell_draw(seeds[12], (D, CHANNELS), D ** -0.5, 0.21875),
        "b_out": bell_draw(seeds[13], (CHANNELS,), 0.5, 3.0, (), jnp.float32),
        "cotangent": bell_draw(seeds[14], (LAT, DATES, LON, SLOT_CHANNELS), 1.0, 6.0, ((2, 8), (3, 4))),
    }


@jax.custom_vjp
def low(v):
    return lax.optimization_barrier(v.astype(jnp.bfloat16)).astype(jnp.float32)

@jax.custom_vjp
def low_back(v):
    return v

def low_keep(v):
    return (low(v), None)

def low_pass(kept, grad):
    return (grad,)

def back_keep(v):
    return (v, None)

def back_low(kept, grad):
    return (low(grad),)
low.defvjp(low_keep, low_pass)
low_back.defvjp(back_keep, back_low)
exact_mode = lax.Precision.HIGHEST

def exact_gelu(values):
    return jax.nn.gelu(values, approximate=False)

def slot_table(levels_of_slots):
    kinds = jnp.arange(SLOT_CHANNELS).astype(jnp.int32) % VARS
    target = jnp.repeat(levels_of_slots.astype(jnp.int32), VARS) * VARS + kinds
    columns = jnp.arange(CHANNELS).astype(jnp.int32)
    return (target[:, None] == columns[None, :]).astype(jnp.float32)

def mlp_block(block, w_one, b_one, w_two, b_two):
    up_values = low_back(jnp.einsum('bcd,df->bcf', block, w_one, precision=exact_mode) + b_one)
    activated = low(exact_gelu(up_values))
    return low_back(jnp.einsum('bcf,fd->bcd', activated, w_two, precision=exact_mode) + b_two)

def forward(table, wet, ocean_state, w_in, b_in, w_depth, norm_gain, norm_bias, w_one, b_one, w_two, b_two, w_out, b_out):
    half = KERNEL // 2
    w_slots = jnp.dot(table, w_in, precision=exact_mode)
    hidden = low_back(jnp.einsum('abcs,sd->abcd', ocean_state, w_slots, precision=exact_mode) + b_in)
    lowered = low(hidden)
    padded = jnp.pad(lowered, ((half, half), (0, 0), (half, half), (0, 0)))
    conv_out = jnp.zeros_like(hidden)
    for tap_row in range(KERNEL):
        for tap_col in range(KERNEL):
            conv_out = conv_out + padded[tap_row:tap_row + LAT, :, tap_col:tap_col + LON, :] * w_depth[tap_row, tap_col]
    conv_out = low_back(conv_out)
    mean_value = lax.optimization_barrier(jnp.mean(conv_out, axis=(0, 1, 2)))
    square_mean = lax.optimization_barrier(jnp.mean(conv_out * conv_out, axis=(0, 1, 2)))
    inv_scale = lax.rsqrt(square_mean - mean_value * mean_value + 1e-05)
    normed = low((conv_out - mean_value) * inv_scale * norm_gain + norm_bias)
    block_fn = jax.checkpoint(partial(mlp_block, w_one=w_one, b_one=b_one, w_two=w_two, b_two=b_two))
    branch = jnp.moveaxis(lax.map(block_fn, jnp.moveaxis(normed, 1, 0)), 0, 1)
    mixed = low((hidden + branch) * wet[:, None, :, None])
    w_out_slots = jnp.dot(w_out, table.T, precision=exact_mode)
    b_slots = jnp.dot(table, b_out, precision=exact_mode)
    return low(jnp.einsum('abcd,ds->abcs', mixed, w_out_slots, precision=exact_mode) + b_slots)

def reference(ocean_state, slot_level, wet_mask, w_in, b_in, w_depth, norm_gain, norm_bias, w_one, b_one, w_two, b_two, w_out, b_out, cotangent):
    table = slot_table(slot_level)
    wet = wet_mask.astype(jnp.float32)
    params = [array.astype(jnp.float32) for array in (ocean_state, w_in, b_in, w_depth, norm_gain, norm_bias, w_one, b_one, w_two, b_two, w_out, b_out)]
    result, pullback = jax.vjp(partial(forward, table, wet), *params)
    grads = pullback(cotangent.astype(jnp.float32))
    return (result.astype(jnp.bfloat16), grads[0].astype(jnp.bfloat16), grads[1], grads[2], grads[3], grads[4], grads[5], grads[6], grads[7], grads[8], grads[9], grads[10], grads[11])
```

```python
import functools

import jax
import jax.numpy as jnp
from jax import lax
from jax.experimental import pallas as pl
from jax.experimental.pallas import tpu as pltpu
from jax.sharding import PartitionSpec as P

VARS = 10
LANES = 128
SUBLANES = 8

exact_mode = lax.Precision.HIGHEST
F32 = jnp.float32
BF16 = jnp.bfloat16

TAIL_SCALE = 0.3
TAIL_POLY = (
    0.119623263,
    0.120845528,
    0.0993471402,
    0.130416391,
    -0.0571672287,
    0.210118226,
    -0.159378204,
    0.0361948279,
)


def slot_table(levels_of_slots, slot_count, channels):
    kinds = jnp.arange(slot_count) % VARS
    target = jnp.repeat(levels_of_slots, VARS) * VARS + kinds
    columns = jnp.arange(channels)
    return (target[:, None] == columns[None, :]).astype(F32)


def bits_of(axis):
    size = lax.axis_size(axis)
    return [(axis, 1 << k) for k in range(size.bit_length() - 1)]


def hop(value, stage):
    axis, bit = stage
    return lax.ppermute(value, axis, [(i, i ^ bit) for i in range(lax.axis_size(axis))])


def side(stage):
    axis, bit = stage
    return (lax.axis_index(axis) // bit) % 2


def butterfly(value, stages):
    for stage in stages:
        value = value + hop(value, stage)
    return value


def reduce_blocks(blocks, stages, link):
    count = blocks.shape[0]
    kept = []
    value = blocks
    own = 0
    for stage in stages:
        if count % 2 == 0:
            half = count // 2
            bit = side(stage)
            sent = lax.dynamic_slice_in_dim(value, (1 - bit) * half, half, 0).astype(link)
            stay = lax.dynamic_slice_in_dim(value, bit * half, half, 0)
            value = stay.astype(F32) + hop(sent, stage).astype(F32)
            kept.append(stage)
            own = own * 2 + bit
            count = half
        else:
            sent = value.astype(link)
            value = sent.astype(F32) + hop(sent, stage).astype(F32)
    value = value.astype(link)
    for stage in reversed(kept):
        value = jnp.concatenate([value, hop(value, stage)], axis=0)
    pieces = 1 << len(kept)
    return [
        lax.dynamic_slice_in_dim(value, (index ^ own) * count, count, 0) for index in range(pieces)
    ]


def hidden_conv_body(rows, cols, half, edge_ref, x_ref, w_ref, b_ref, depth_ref, hidden_ref, low_ref, conv_ref, stat_ref, pad_ref):
    kernel = 2 * half + 1
    value = jnp.dot(x_ref[...], w_ref[...], preferred_element_type=F32) + b_ref[...]
    value = value.reshape(rows + 2 * half, cols + 2 * half, SUBLANES, LANES)
    hidden_ref[...] = value[half : half + rows, half : half + cols]
    pad_ref[...] = value.astype(BF16).astype(F32)

    @pl.when(edge_ref[0] == 1)
    def _():
        pad_ref[:half] = jnp.zeros((half,) + pad_ref.shape[1:], F32)

    @pl.when(edge_ref[1] == 1)
    def _():
        pad_ref[half + rows :] = jnp.zeros((half,) + pad_ref.shape[1:], F32)

    @pl.when(edge_ref[2] == 1)
    def _():
        pad_ref[:, :half] = jnp.zeros((pad_ref.shape[0], half) + pad_ref.shape[2:], F32)

    @pl.when(edge_ref[3] == 1)
    def _():
        pad_ref[:, half + cols :] = jnp.zeros((pad_ref.shape[0], half) + pad_ref.shape[2:], F32)

    low_ref[...] = pad_ref[...].reshape(low_ref.shape).astype(BF16)

    def one_row(row, carry):
        total, square = carry
        acc = jnp.zeros((cols, SUBLANES, LANES), F32)
        for i in range(kernel):
            slab = pad_ref[row + i]
            for j in range(kernel):
                acc = acc + slab[j : j + cols] * depth_ref[i * kernel + j]
        conv_ref[row] = acc
        return total + jnp.sum(acc, axis=0), square + jnp.sum(acc * acc, axis=0)

    zero = jnp.zeros((SUBLANES, LANES), F32)
    total, square = lax.fori_loop(0, rows, one_row, (zero, zero))
    stat_ref[0:1] = jnp.sum(total, axis=0, keepdims=True)
    stat_ref[1:2] = jnp.sum(square, axis=0, keepdims=True)


def hidden_conv(edges, x, w_slots, b_in, depth, tile):
    rows, cols, dates, half = tile
    width = w_slots.shape[1]
    padded = (rows + 2 * half) * (cols + 2 * half) * dates
    slots = x.shape[1]
    grid = pl.cdiv(width, LANES)
    return pl.pallas_call(
        functools.partial(hidden_conv_body, rows, cols, half),
        grid=(grid,),
        in_specs=[
            pl.BlockSpec(memory_space=pltpu.SMEM),
            pl.BlockSpec((padded, slots), lambda i: (0, 0)),
            pl.BlockSpec((slots, LANES), lambda i: (0, i)),
            pl.BlockSpec((1, LANES), lambda i: (0, i)),
            pl.BlockSpec((depth.shape[0], 1, LANES), lambda i: (0, 0, i)),
        ],
        out_specs=[
            pl.BlockSpec((rows, cols, dates, LANES), lambda i: (0, 0, 0, i)),
            pl.BlockSpec((padded, LANES), lambda i: (0, i)),
            pl.BlockSpec((rows, cols, dates, LANES), lambda i: (0, 0, 0, i)),
            pl.BlockSpec((2, LANES), lambda i: (0, i)),
        ],
        out_shape=[
            jax.ShapeDtypeStruct((rows, cols, dates, width), F32),
            jax.ShapeDtypeStruct((padded, width), BF16),
            jax.ShapeDtypeStruct((rows, cols, dates, width), F32),
            jax.ShapeDtypeStruct((2, width), F32),
        ],
        scratch_shapes=[pltpu.VMEM((rows + 2 * half, cols + 2 * half, dates, LANES), F32)],
        name="hidden_conv",
    )(edges, x, w_slots, b_in.reshape(1, -1), depth)


def gelu_pair(values):
    size = jnp.abs(values)
    gauss = jnp.exp(-0.5 * values * values)
    t = 1.0 / (1.0 + TAIL_SCALE * size)
    poly = jnp.full_like(t, TAIL_POLY[-1])
    for factor in TAIL_POLY[-2::-1]:
        poly = poly * t + factor
    tail = gauss * (t * poly)
    below = jnp.where(values >= 0, 1.0 - tail, tail)
    return values * below, below + values * (gauss * 0.3989422804014327)


def mlp_body(row_block, normed_ref, branch_ref, w_one_ref, b_one_ref, w_two_ref, act_ref, dup_ref, grad_ref, gb_ref, normed_t, branch_t):
    @pl.when(pl.program_id(0) == 0)
    def _():
        normed_t[...] = normed_ref[...].T
        branch_t[...] = branch_ref[...].T

    total = jnp.zeros((1, act_ref.shape[1]), F32)
    for start in range(0, normed_ref.shape[0], row_block):
        rows = pl.ds(start, row_block)
        up = jnp.dot(normed_ref[rows], w_one_ref[...], preferred_element_type=F32) + b_one_ref[...]
        d_act = lax.dot_general(
            branch_ref[rows], w_two_ref[...], (((1,), (1,)), ((), ())), preferred_element_type=F32
        )
        value, slope = gelu_pair(up)
        act_ref[rows] = value.astype(BF16)
        d_up = (slope * d_act).astype(BF16)
        dup_ref[rows] = d_up
        total = total + jnp.sum(d_up.astype(F32), axis=0, keepdims=True)
    gb_ref[...] = total
    grad_ref[0] = jnp.dot(normed_t[...], dup_ref[...], preferred_element_type=F32).astype(BF16)
    grad_ref[1] = jnp.dot(branch_t[...], act_ref[...], preferred_element_type=F32).astype(BF16)


def mlp(normed, d_branch, w_one, b_one, w_two, block=256, row_block=256):
    pixels, width = normed.shape
    hidden = w_one.shape[1]
    return pl.pallas_call(
        functools.partial(mlp_body, row_block),
        grid=(pl.cdiv(hidden, block),),
        in_specs=[
            pl.BlockSpec((pixels, width), lambda i: (0, 0)),
            pl.BlockSpec((pixels, width), lambda i: (0, 0)),
            pl.BlockSpec((width, block), lambda i: (0, i)),
            pl.BlockSpec((1, block), lambda i: (0, i)),
            pl.BlockSpec((block, width), lambda i: (i, 0)),
        ],
        out_specs=[
            pl.BlockSpec((pixels, block), lambda i: (0, i)),
            pl.BlockSpec((pixels, block), lambda i: (0, i)),
            pl.BlockSpec((2, width, block), lambda i: (0, 0, i)),
            pl.BlockSpec((1, block), lambda i: (0, i)),
        ],
        out_shape=[
            jax.ShapeDtypeStruct((pixels, hidden), BF16),
            jax.ShapeDtypeStruct((pixels, hidden), BF16),
            jax.ShapeDtypeStruct((2, width, hidden), BF16),
            jax.ShapeDtypeStruct((1, hidden), F32),
        ],
        scratch_shapes=[pltpu.VMEM((width, pixels), BF16), pltpu.VMEM((width, pixels), BF16)],
        name="mlp",
    )(normed, d_branch, w_one, b_one.reshape(1, -1), w_two)


def conv_back_body(rows, cols, half, edge_ref, coef_ref, dn_ref, conv_ref, dsum_ref, low_ref, depth_ref, dh_ref, gw_ref, gb_ref, dc_ref, dl_ref, pad_ref, tap_ref):
    kernel = 2 * half + 1
    wide = cols + 2 * half
    d_conv = coef_ref[0:1] * dn_ref[...] + (coef_ref[1:2] * conv_ref[...] + coef_ref[2:3])
    dc_ref[...] = d_conv.astype(BF16).astype(F32)
    dl_ref[...] = jnp.zeros(dl_ref.shape, F32)
    dl_ref[half : half + rows, half : half + cols] = dsum_ref[...]
    pad_ref[...] = low_ref[...].astype(F32).reshape(pad_ref.shape)
    tap_ref[...] = jnp.zeros(tap_ref.shape, F32)

    def one_row(row, carry):
        source = [dc_ref[row, c] for c in range(cols)]
        for i in range(kernel):
            taps = [jnp.broadcast_to(depth_ref[i * kernel + j], (SUBLANES, LANES)) for j in range(kernel)]
            for c in range(wide):
                acc = dl_ref[row + i, c]
                for j in range(kernel):
                    if 0 <= c - j < cols:
                        acc = acc + source[c - j] * taps[j]
                dl_ref[row + i, c] = acc
        for i in range(kernel):
            sums = [tap_ref[i * kernel + j] for j in range(kernel)]
            for c in range(wide):
                value = pad_ref[row + i, c]
                for j in range(kernel):
                    if 0 <= c - j < cols:
                        sums[j] = sums[j] + source[c - j] * value
            for j in range(kernel):
                tap_ref[i * kernel + j] = sums[j]
        return carry

    lax.fori_loop(0, rows, one_row, 0)

    @pl.when(edge_ref[0] == 1)
    def _():
        dl_ref[:half] = jnp.zeros((half,) + dl_ref.shape[1:], F32)

    @pl.when(edge_ref[1] == 1)
    def _():
        dl_ref[half + rows :] = jnp.zeros((half,) + dl_ref.shape[1:], F32)

    @pl.when(edge_ref[2] == 1)
    def _():
        dl_ref[:, :half] = jnp.zeros((dl_ref.shape[0], half) + dl_ref.shape[2:], F32)

    @pl.when(edge_ref[3] == 1)
    def _():
        dl_ref[:, half + cols :] = jnp.zeros((dl_ref.shape[0], half) + dl_ref.shape[2:], F32)

    d_hidden = dl_ref[...]
    dh_ref[...] = d_hidden.reshape(dh_ref.shape).astype(BF16)
    gb_ref[...] = jnp.sum(jnp.sum(d_hidden, axis=(0, 1)), axis=0, keepdims=True)
    gw_ref[...] = jnp.sum(tap_ref[...], axis=1)


def conv_back(edges, coef, d_normed, conv_out, d_sum, lowered, depth, tile):
    rows, cols, dates, half = tile
    taps = depth.shape[0]
    width = lowered.shape[1]
    padded = lowered.shape[0]
    inner = pl.BlockSpec((rows, cols, dates, LANES), lambda i: (0, 0, 0, i))
    wide = (rows + 2 * half, cols + 2 * half, dates, LANES)
    return pl.pallas_call(
        functools.partial(conv_back_body, rows, cols, half),
        grid=(pl.cdiv(width, LANES),),
        in_specs=[
            pl.BlockSpec(memory_space=pltpu.SMEM),
            pl.BlockSpec((3, LANES), lambda i: (0, i)),
            inner,
            inner,
            inner,
            pl.BlockSpec((padded, LANES), lambda i: (0, i)),
            pl.BlockSpec((taps, 1, LANES), lambda i: (0, 0, i)),
        ],
        out_specs=[
            pl.BlockSpec((padded, LANES), lambda i: (0, i)),
            pl.BlockSpec((taps, LANES), lambda i: (0, i)),
            pl.BlockSpec((1, LANES), lambda i: (0, i)),
        ],
        out_shape=[
            jax.ShapeDtypeStruct((padded, width), BF16),
            jax.ShapeDtypeStruct((taps, width), F32),
            jax.ShapeDtypeStruct((1, width), F32),
        ],
        scratch_shapes=[
            pltpu.VMEM((rows, cols, dates, LANES), F32),
            pltpu.VMEM(wide, F32),
            pltpu.VMEM(wide, F32),
            pltpu.VMEM((taps, dates, LANES), F32),
        ],
        name="conv_back",
    )(edges, coef, d_normed, conv_out, d_sum, lowered, depth)


def on_device(
    ocean_state,
    slot_level,
    wet_mask,
    w_in,
    b_in,
    w_depth,
    norm_gain,
    norm_bias,
    w_one,
    b_one,
    w_two,
    b_two,
    w_out,
    b_out,
    cotangent,
):
    groups = lax.axis_size("lev")
    strips = lax.axis_size("sp")
    group_index = lax.axis_index("lev")
    strip_index = lax.axis_index("sp")
    rows, cols = wet_mask.shape
    all_rows, dates, _, group_ch = ocean_state.shape
    slots = group_ch * groups
    channels, width = w_in.shape
    kernel = w_depth.shape[0]
    half = kernel // 2
    tile = (rows, cols, dates, half)
    high_rows, wide_cols = rows + 2 * half, cols + 2 * half
    pixels = rows * cols * dates
    pixel_total = float(pixels * groups * strips)

    lev_stages = bits_of("lev")
    sp_stages = bits_of("sp")
    stages = lev_stages + sp_stages
    core, lev_rest = lev_stages[:1], lev_stages[1:]
    orders = (
        core + lev_rest + sp_stages,
        core + sp_stages[:1] + lev_rest + sp_stages[1:],
        core + sp_stages[1:2] + lev_rest + sp_stages[:1] + sp_stages[2:],
    )
    forward = [(i, i + 1) for i in range(strips - 1)]
    backward = [(i + 1, i) for i in range(strips - 1)]
    edges = jnp.stack(
        [group_index == 0, group_index == groups - 1, strip_index == 0, strip_index == strips - 1]
    ).astype(jnp.int32)

    table = slot_table(slot_level, slots, channels)
    table_low = table.astype(BF16)
    w_slots = jnp.dot(table_low, w_in, preferred_element_type=F32).astype(BF16)
    w_out_slots = jnp.dot(w_out, table_low.T, preferred_element_type=F32).astype(BF16)
    b_slots = jnp.dot(table, b_out, precision=exact_mode)
    depth = w_depth.astype(F32).reshape(kernel * kernel, 1, width)

    state = ocean_state.transpose(0, 2, 1, 3).reshape(all_rows, cols, dates * group_ch)
    low_cols = lax.ppermute(state[:, cols - half :], "sp", forward)
    high_cols = lax.ppermute(state[:, :half], "sp", backward)
    state = jnp.concatenate([low_cols, state, high_cols], axis=1)
    state = jnp.pad(state, ((half, half), (0, 0), (0, 0)))
    windows = jnp.stack([state[g * rows : g * rows + high_rows] for g in range(groups)])
    windows = lax.all_to_all(windows, "lev", split_axis=0, concat_axis=0, tiled=True)
    x_pad = (
        windows.reshape(groups, high_rows, wide_cols, dates, group_ch)
        .transpose(1, 2, 3, 0, 4)
        .reshape(high_rows * wide_cols * dates, slots)
    )
    d_result = cotangent.transpose(0, 2, 1, 3).reshape(groups, rows, cols, dates * group_ch)
    d_result = lax.all_to_all(d_result, "lev", split_axis=0, concat_axis=0, tiled=True)
    d_result = (
        d_result.reshape(groups, rows, cols, dates, group_ch)
        .transpose(1, 2, 3, 0, 4)
        .reshape(pixels, slots)
    )

    hidden, lowered, conv_out, local = hidden_conv(edges, x_pad, w_slots, b_in, depth, tile)
    total = butterfly(local, stages)
    wet = jnp.broadcast_to(
        wet_mask.astype(F32)[:, :, None, None], (rows, cols, dates, 1)
    ).reshape(pixels, 1)
    d_mixed = jnp.dot(d_result, w_out_slots.T, preferred_element_type=F32)
    d_sum = d_mixed * wet
    d_branch = d_sum.astype(BF16)
    g_b_two = jnp.sum(d_branch.astype(F32), axis=0)
    g_bias_slots = jnp.sum(d_result.astype(F32), axis=0)

    mean_value = total[0] / pixel_total
    inv_scale = lax.rsqrt(total[1] / pixel_total - mean_value * mean_value + 1e-05)
    conv_flat = conv_out.reshape(pixels, width)
    centered = (conv_flat - mean_value) * inv_scale
    normed = (centered * norm_gain + norm_bias).astype(BF16)
    activated, d_up, grads, g_b_one = mlp(normed, d_branch, w_one, b_one, w_two)

    ff = w_one.shape[1]
    cuts = [0, min(1280, ff), min(2560, ff), ff]
    reduced = []
    for order, low, high in zip(orders, cuts[:-1], cuts[1:]):
        blocks = grads[:, :, low:high].reshape(2 * width // SUBLANES, SUBLANES, high - low)
        pieces = reduce_blocks(blocks, order, BF16)
        reduced.append(jnp.concatenate(pieces, axis=0).reshape(2, width, high - low))
    grad_w_one = jnp.concatenate([r[0] for r in reduced], axis=1).astype(F32)
    grad_w_two = jnp.concatenate([r[1].T for r in reduced], axis=0).astype(F32)

    d_normed = lax.dot_general(
        d_up, w_one, (((1,), (1,)), ((), ())), preferred_element_type=F32
    )
    parts = jnp.stack([jnp.sum(d_normed, axis=0), jnp.sum(d_normed * centered, axis=0)])
    norm_grads = butterfly(parts, stages)
    branch = jnp.dot(activated, w_two, preferred_element_type=F32) + b_two
    mixed = ((hidden.reshape(pixels, width) + branch) * wet).astype(BF16)
    result = (jnp.dot(mixed, w_out_slots, preferred_element_type=F32) + b_slots).astype(BF16)
    result = result.reshape(rows, cols, dates, groups, group_ch).transpose(3, 0, 1, 2, 4)
    result = result.reshape(groups, rows, cols, dates * group_ch)
    next_state = lax.all_to_all(result, "lev", split_axis=0, concat_axis=0, tiled=True)
    next_state = next_state.reshape(all_rows, cols, dates, group_ch).transpose(0, 2, 1, 3)
    g_out_slots = lax.dot_general(
        d_result, mixed, (((0,), (0,)), ((), ())), preferred_element_type=F32
    )

    scale = norm_gain * inv_scale
    slope = scale * inv_scale * (norm_grads[1] / pixel_total)
    coef = jnp.stack(
        [scale, -slope, slope * mean_value - scale * (norm_grads[0] / pixel_total)]
    )
    shape4 = (rows, cols, dates, width)
    d_hidden, g_w_depth, g_b_in = conv_back(
        edges, coef, d_normed.reshape(shape4), conv_out, d_sum.reshape(shape4), lowered, depth, tile
    )
    d_state = lax.dot_general(
        d_hidden, w_slots, (((1,), (1,)), ((), ())), preferred_element_type=F32
    ).reshape(high_rows, wide_cols, dates, slots)
    g_in_slots = lax.dot_general(
        x_pad, d_hidden, (((0,), (0,)), ((), ())), preferred_element_type=F32
    )
    to_low = lax.ppermute(d_state[:, :half].astype(BF16), "sp", backward)
    to_high = lax.ppermute(d_state[:, half + cols :].astype(BF16), "sp", forward)
    d_state = d_state[:, half : half + cols]
    d_state = d_state + jnp.pad(
        to_low.astype(F32), ((0, 0), (cols - half, 0), (0, 0), (0, 0))
    )
    d_state = d_state + jnp.pad(
        to_high.astype(F32), ((0, 0), (0, cols - half), (0, 0), (0, 0))
    )
    d_state = (
        d_state.astype(BF16)
        .reshape(high_rows, cols, dates, groups, group_ch)
        .transpose(3, 0, 1, 2, 4)
        .reshape(groups, high_rows, cols, dates * group_ch)
    )
    d_state = lax.all_to_all(d_state, "lev", split_axis=0, concat_axis=0, tiled=True).astype(F32)
    inner = d_state[:, half : half + rows]
    inner = inner + jnp.pad(
        d_state[:-1, half + rows :], ((1, 0), (0, rows - half), (0, 0), (0, 0))
    )
    inner = inner + jnp.pad(d_state[1:, :half], ((0, 1), (rows - half, 0), (0, 0), (0, 0)))
    grad_ocean_state = (
        inner.astype(BF16).reshape(all_rows, cols, dates, group_ch).transpose(0, 2, 1, 3)
    )

    def as_rows(vector):
        flat = vector.reshape(-1)
        count = -(-flat.shape[0] // width)
        return jnp.pad(flat, (0, count * width - flat.shape[0])).reshape(count, width)

    def summed(arrays, order):
        packed = jnp.concatenate(arrays, axis=0)
        count = packed.shape[0]
        unit = 16 * SUBLANES
        packed = jnp.pad(packed, ((0, -count % unit), (0, 0)))
        pieces = reduce_blocks(packed.reshape(-1, SUBLANES, width), order, F32)
        packed = jnp.concatenate(pieces, axis=0).reshape(-1, width)
        found = []
        start = 0
        for array in arrays:
            found.append(packed[start : start + array.shape[0]])
            start += array.shape[0]
        return found

    early = summed(
        [g_out_slots, as_rows(g_b_one), as_rows(g_b_two), as_rows(g_bias_slots)], orders[0]
    )
    late = summed([g_in_slots, g_w_depth, g_b_in], orders[0])
    grad_w_out = jnp.einsum("sd,sc->dc", early[0], table, precision=exact_mode)
    grad_b_one = early[1].reshape(-1)[:ff]
    grad_b_two = early[2].reshape(-1)
    grad_b_out = jnp.dot(early[3].reshape(-1)[:slots], table, precision=exact_mode)
    grad_w_in = jnp.dot(table.T, late[0], precision=exact_mode)
    grad_w_depth = late[1].reshape(kernel, kernel, width)
    grad_b_in = late[2].reshape(-1)
    return (
        next_state,
        grad_ocean_state,
        grad_w_in,
        grad_b_in,
        grad_w_depth,
        norm_grads[1],
        norm_grads[0],
        grad_w_one,
        grad_b_one,
        grad_w_two,
        grad_b_two,
        grad_w_out,
        grad_b_out,
    )


def solution(mesh):
    return jax.shard_map(
        on_device,
        mesh=mesh,
        in_specs=(
            P(None, None, "sp", "lev"),
            P(),
            P("lev", "sp"),
            P(),
            P(),
            P(),
            P(),
            P(),
            P(),
            P(),
            P(),
            P(),
            P(),
            P(),
            P(None, None, "sp", "lev"),
        ),
        out_specs=(
            P(None, None, "sp", "lev"),
            P(None, None, "sp", "lev"),
            P(),
            P(),
            P(),
            P(),
            P(),
            P(),
            P(),
            P(),
            P(),
            P(),
            P(),
        ),
        check_vma=False,
    )
```

```python
import functools

import jax
import jax.numpy as jnp
from jax import lax
from jax.experimental import pallas as pl
from jax.experimental.pallas import tpu as pltpu
from jax.sharding import PartitionSpec as P

VARS = 10
LANES = 128
SUBLANES = 8

exact_mode = lax.Precision.HIGHEST
F32 = jnp.float32
BF16 = jnp.bfloat16

TAIL_SCALE = 0.3
TAIL_POLY = (
    0.119623263,
    0.120845528,
    0.0993471402,
    0.130416391,
    -0.0571672287,
    0.210118226,
    -0.159378204,
    0.0361948279,
)


def slot_table(levels_of_slots, groups, group_ch, padded_ch, channels):
    slot_count = groups * group_ch
    kinds = jnp.arange(slot_count) % VARS
    target = jnp.repeat(levels_of_slots, VARS) * VARS + kinds
    target = jnp.pad(
        target.reshape(groups, group_ch), ((0, 0), (0, padded_ch - group_ch)), constant_values=-1
    ).reshape(-1)
    columns = jnp.arange(channels)
    return (target[:, None] == columns[None, :]).astype(F32)


def bits_of(axis):
    size = lax.axis_size(axis)
    return [(axis, 1 << k) for k in range(size.bit_length() - 1)]


def hop(value, stage):
    axis, bit = stage
    return lax.ppermute(value, axis, [(i, i ^ bit) for i in range(lax.axis_size(axis))])


def side(stage):
    axis, bit = stage
    return (lax.axis_index(axis) // bit) % 2


def butterfly(value, stages):
    for stage in stages:
        value = value + hop(value, stage)
    return value


def after(value, *earlier):
    return lax.optimization_barrier((value,) + earlier)[0]


def halves(value, axis, bit):
    half = value.shape[axis] // 2
    stay = lax.dynamic_slice_in_dim(value, bit * half, half, axis)
    sent = lax.dynamic_slice_in_dim(value, (1 - bit) * half, half, axis)
    return stay, sent


def halving_lanes(lanes):
    return lanes % (2 * LANES) == 0


def total(terms):
    value = terms[0].astype(F32)
    for term in terms[1:]:
        value = value + term.astype(F32)
    return value


def exchange(value, stages, link, partner=None, most=2):
    kept = []
    own = 0
    terms = [value]
    rest = stages
    if partner is not None:
        came = hop(partner, stages[0])
        token = yield partner
        terms.append(after(came, token))
        rest = stages[1:]
    row_halvings = 0
    for stage in rest:
        bit = side(stage)
        shape = terms[0].shape
        if stage is rest[-1]:
            axis = None
        elif shape[0] % 2 == 0 and row_halvings < most:
            axis = 0
            row_halvings += 1
            own = own * 2 + bit
        else:
            axis = 2 if halving_lanes(shape[2]) else None
        if axis is None:
            sent = total(terms).astype(link)
            terms = [sent]
        else:
            pairs = [halves(term, axis, bit) for term in terms]
            sent = total([pair[1] for pair in pairs]).astype(link)
            terms = [pair[0] for pair in pairs]
            kept.append((stage, axis))
        came = hop(sent, stage)
        token = yield sent
        terms.append(after(came, token))
    value = total(terms).astype(link)
    for stage, axis in reversed(kept):
        came = hop(value, stage)
        token = yield value
        came = after(came, token)
        if axis == 0:
            value = jnp.concatenate([value, came], axis=0)
        else:
            bit = side(stage)
            low = jnp.where(bit == 0, value, came)
            high = jnp.where(bit == 0, came, value)
            value = jnp.concatenate([low, high], axis=2)
    other = None
    if partner is not None:
        came = hop(value, stages[0])
        token = yield value
        other = after(came, token)
    yield value, other, own, 1 << row_halvings


def in_order(value, other, own, pieces):
    count = value.shape[0] // pieces
    return jnp.concatenate(
        [lax.dynamic_slice_in_dim(value, (index ^ own) * count, count, 0) for index in range(pieces)],
        axis=0,
    )


class Exchanges:
    def __init__(self):
        self.running = {}
        self.done = {}

    def begin(self, name, *args, **options):
        self.running[name] = exchange(*args, **options)
        return next(self.running[name])

    def step(self, token, *names):
        sent = []
        for name in names:
            if name in self.running:
                got = self.running[name].send(token)
                if isinstance(got, tuple):
                    self.done[name] = got
                    del self.running[name]
                else:
                    sent.append(got)
        return sent

    def finish(self, token, *names):
        while any(name in self.running for name in names):
            self.step(token, *names)


def unpack_grads(core_side, reduced, width, ff, start, prior=()):
    value, other, own, pieces = reduced
    count = value.shape[0] // pieces
    rows = count * SUBLANES
    columns = value.shape[2]

    def body(own_ref, value_ref, other_ref, *refs):
        out_one, out_two = refs[len(prior) :]
        mine = value_ref[...].astype(F32).reshape(rows, columns)
        theirs = other_ref[...].astype(F32).reshape(rows, columns)
        first = own_ref[1] == 0

        @pl.when(first)
        def _():
            out_one[...] = mine
            out_two[...] = theirs

        @pl.when(jnp.logical_not(first))
        def _():
            out_one[...] = theirs
            out_two[...] = mine

    out = pl.BlockSpec((pl.Element(rows), pl.Element(columns)), lambda i, own: (i * rows, start))
    piece = pl.BlockSpec((count, SUBLANES, columns), lambda i, own: (i ^ own[0], 0, 0))
    return pl.pallas_call(
        body,
        grid_spec=pltpu.PrefetchScalarGridSpec(
            num_scalar_prefetch=1,
            grid=(pieces,),
            in_specs=[piece, piece] + [pl.BlockSpec(memory_space=pl.ANY)] * len(prior),
            out_specs=[out, out],
        ),
        out_shape=[jax.ShapeDtypeStruct((width, ff), F32)] * 2,
        input_output_aliases={3 + k: k for k in range(len(prior))},
        name="unpack_grads",
    )(jnp.stack([own, core_side]).astype(jnp.int32), value, other, *prior)


def pixel_order(dates, cols):
    pixels = dates * cols
    source = lax.broadcasted_iota(jnp.int32, (pixels, pixels), 0)
    place = lax.broadcasted_iota(jnp.int32, (pixels, pixels), 1)
    return ((source % cols) * dates + source // cols == place).astype(BF16)


def to_channel_rows(state, cotangent, groups, half, padded_ch):
    all_rows, dates, cols, ch = state.shape
    rows = all_rows // groups
    high = rows + 2 * half
    pixels = dates * cols

    def body(state_ref, cot_ref, window_ref, ct_ref):
        perm = pixel_order(dates, cols)
        blank = jnp.zeros((padded_ch - ch, pixels), F32)
        zero = jnp.zeros((padded_ch, pixels), BF16)

        def turned(ref, row):
            value = lax.dot_general(
                ref[row].reshape(pixels, ch), perm, (((0,), (0,)), ((), ())), preferred_element_type=F32
            )
            return jnp.concatenate([value, blank], axis=0).astype(BF16) if padded_ch > ch else value.astype(BF16)

        for row in range(half):
            window_ref[0, row] = zero
            window_ref[groups - 1, half + rows + row] = zero
        for row in range(all_rows):
            value = turned(state_ref, row)
            for band in range(groups):
                place = row - band * rows + half
                if 0 <= place < high:
                    window_ref[band, place] = value
            ct_ref[row // rows, row % rows] = turned(cot_ref, row)

    return pl.pallas_call(
        body,
        out_shape=[
            jax.ShapeDtypeStruct((groups, high, padded_ch, pixels), BF16),
            jax.ShapeDtypeStruct((groups, rows, padded_ch, pixels), BF16),
        ],
        name="to_channel_rows",
    )(state, cotangent)


def from_channel_rows(windows, half, dates, cols, ch):
    groups, high, padded_ch, pixels = windows.shape
    rows = high - 2 * half

    def body(window_ref, out_ref):
        perm = pixel_order(dates, cols)
        for row in range(groups * rows):
            value = None
            for band in range(groups):
                place = row - band * rows + half
                if 0 <= place < high:
                    piece = window_ref[band, place]
                    value = piece if value is None else value.astype(F32) + piece.astype(F32)
            value = lax.dot_general(
                perm, value.astype(BF16), (((1,), (1,)), ((), ())), preferred_element_type=F32
            )
            out_ref[row] = value[:, :ch].astype(BF16).reshape(dates, cols, ch)

    return pl.pallas_call(
        body,
        out_shape=jax.ShapeDtypeStruct((groups * rows, dates, cols, ch), BF16),
        name="from_channel_rows",
    )(windows)


def to_pixel_rows(received):
    groups, rows, padded_ch, pixels = received.shape
    slots = groups * padded_ch

    def body(in_ref, out_ref):
        for row in range(rows):
            value = jnp.concatenate([in_ref[g, row].astype(F32) for g in range(groups)], axis=0)
            out_ref[row] = value.T.astype(BF16)

    return pl.pallas_call(
        body,
        out_shape=jax.ShapeDtypeStruct((rows, pixels, slots), BF16),
        name="to_pixel_rows",
    )(received)


def hidden_conv_body(rows, cols, half, edge_ref, x_ref, low_x_ref, high_x_ref, w_ref, b_ref, depth_ref, hidden_ref, low_ref, conv_ref, stat_ref, pad_ref):
    kernel = 2 * half + 1
    high = rows + 2 * half

    def hidden_of(ref, columns):
        value = jnp.dot(ref[...], w_ref[...], preferred_element_type=F32) + b_ref[...]
        return value.reshape(high, columns, SUBLANES, LANES)

    value = hidden_of(x_ref, cols)
    hidden_ref[...] = value[half : half + rows]
    pad_ref[:, half : half + cols] = value.astype(BF16).astype(F32)
    pad_ref[:, :half] = hidden_of(low_x_ref, half).astype(BF16).astype(F32)
    pad_ref[:, half + cols :] = hidden_of(high_x_ref, half).astype(BF16).astype(F32)

    @pl.when(edge_ref[0] == 1)
    def _():
        pad_ref[:half] = jnp.zeros((half,) + pad_ref.shape[1:], F32)

    @pl.when(edge_ref[1] == 1)
    def _():
        pad_ref[half + rows :] = jnp.zeros((half,) + pad_ref.shape[1:], F32)

    @pl.when(edge_ref[2] == 1)
    def _():
        pad_ref[:, :half] = jnp.zeros((pad_ref.shape[0], half) + pad_ref.shape[2:], F32)

    @pl.when(edge_ref[3] == 1)
    def _():
        pad_ref[:, half + cols :] = jnp.zeros((pad_ref.shape[0], half) + pad_ref.shape[2:], F32)

    low_ref[...] = pad_ref[...].reshape(low_ref.shape).astype(BF16)

    def one_row(row, carry):
        total, square = carry
        acc = jnp.zeros((cols, SUBLANES, LANES), F32)
        for i in range(kernel):
            slab = pad_ref[row + i]
            for j in range(kernel):
                acc = acc + slab[j : j + cols] * depth_ref[i * kernel + j]
        conv_ref[row] = acc
        return total + jnp.sum(acc, axis=0), square + jnp.sum(acc * acc, axis=0)

    zero = jnp.zeros((SUBLANES, LANES), F32)
    total, square = lax.fori_loop(0, rows, one_row, (zero, zero))
    stat_ref[0:1] = jnp.sum(total, axis=0, keepdims=True)
    stat_ref[1:2] = jnp.sum(square, axis=0, keepdims=True)


def hidden_conv(edges, x, low_x, high_x, w_slots, b_in, depth, tile):
    rows, cols, dates, half = tile
    slots, width = w_slots.shape
    padded = (rows + 2 * half) * (cols + 2 * half) * dates
    return pl.pallas_call(
        functools.partial(hidden_conv_body, rows, cols, half),
        grid=(pl.cdiv(width, LANES),),
        in_specs=[
            pl.BlockSpec(memory_space=pltpu.SMEM),
            pl.BlockSpec(x.shape, lambda i: (0, 0)),
            pl.BlockSpec(low_x.shape, lambda i: (0, 0)),
            pl.BlockSpec(high_x.shape, lambda i: (0, 0)),
            pl.BlockSpec((slots, LANES), lambda i: (0, i)),
            pl.BlockSpec((1, LANES), lambda i: (0, i)),
            pl.BlockSpec((depth.shape[0], 1, LANES), lambda i: (0, 0, i)),
        ],
        out_specs=[
            pl.BlockSpec((rows, cols, dates, LANES), lambda i: (0, 0, 0, i)),
            pl.BlockSpec((padded, LANES), lambda i: (0, i)),
            pl.BlockSpec((rows, cols, dates, LANES), lambda i: (0, 0, 0, i)),
            pl.BlockSpec((2, LANES), lambda i: (0, i)),
        ],
        out_shape=[
            jax.ShapeDtypeStruct((rows, cols, dates, width), F32),
            jax.ShapeDtypeStruct((padded, width), BF16),
            jax.ShapeDtypeStruct((rows, cols, dates, width), F32),
            jax.ShapeDtypeStruct((2, width), F32),
        ],
        scratch_shapes=[pltpu.VMEM((rows + 2 * half, cols + 2 * half, dates, LANES), F32)],
        cost_estimate=pl.CostEstimate(
            flops=20000000000, transcendentals=0, bytes_accessed=20 * padded * width
        ),
        name="hidden_conv",
    )(edges, x, low_x, high_x, w_slots, b_in.reshape(1, -1), depth)


def gelu_pair(values):
    size = jnp.abs(values)
    gauss = jnp.exp(-0.5 * values * values)
    t = 1.0 / (1.0 + TAIL_SCALE * size)
    poly = jnp.full_like(t, TAIL_POLY[-1])
    for factor in TAIL_POLY[-2::-1]:
        poly = poly * t + factor
    tail = gauss * (t * poly)
    below = jnp.where(values >= 0, 1.0 - tail, tail)
    return values * below, below + values * (gauss * 0.3989422804014327)


def mlp_body(row_block, core_ref, normed_ref, branch_ref, w_one_ref, b_one_ref, w_two_ref, act_ref, dup_ref, keep_ref, send_ref, gb_ref, normed_t, branch_t):
    @pl.when(pl.program_id(0) == 0)
    def _():
        normed_t[...] = normed_ref[...].T
        branch_t[...] = branch_ref[...].T

    total = jnp.zeros((1, act_ref.shape[1]), F32)
    for start in range(0, normed_ref.shape[0], row_block):
        rows = pl.ds(start, row_block)
        up = jnp.dot(normed_ref[rows], w_one_ref[...], preferred_element_type=F32) + b_one_ref[...]
        d_act = jnp.dot(branch_ref[rows], w_two_ref[...], preferred_element_type=F32)
        value, slope = gelu_pair(up)
        act_ref[rows] = value.astype(BF16)
        d_up = (slope * d_act).astype(BF16)
        dup_ref[rows] = d_up
        total = total + jnp.sum(d_up.astype(F32), axis=0, keepdims=True)
    gb_ref[...] = total
    grad_one = jnp.dot(normed_t[...], dup_ref[...], preferred_element_type=F32).astype(BF16)
    grad_two = jnp.dot(branch_t[...], act_ref[...], preferred_element_type=F32).astype(BF16)
    first = core_ref[0] == 0

    @pl.when(first)
    def _():
        keep_ref[...] = grad_one
        send_ref[...] = grad_two

    @pl.when(jnp.logical_not(first))
    def _():
        keep_ref[...] = grad_two
        send_ref[...] = grad_one


def mlp(core_side, normed, d_branch, w_one, b_one, w_two, first, last, prior=(), block=256, row_block=256):
    pixels, width = normed.shape
    hidden = w_one.shape[1]
    start = first // block

    def body(core_ref, normed_ref, branch_ref, w_one_ref, b_one_ref, w_two_ref, *refs):
        mlp_body(row_block, core_ref, normed_ref, branch_ref, w_one_ref, b_one_ref, w_two_ref, *refs[len(prior) :])

    whole = jax.ShapeDtypeStruct((pixels, hidden), BF16)
    grad = jax.ShapeDtypeStruct((width, last - first), BF16)
    results = pl.pallas_call(
        body,
        grid=(pl.cdiv(last - first, block),),
        in_specs=[
            pl.BlockSpec(memory_space=pltpu.SMEM),
            pl.BlockSpec((pixels, width), lambda i: (0, 0)),
            pl.BlockSpec((pixels, width), lambda i: (0, 0)),
            pl.BlockSpec((width, block), lambda i: (0, start + i)),
            pl.BlockSpec((1, block), lambda i: (0, start + i)),
            pl.BlockSpec((width, block), lambda i: (0, start + i)),
        ]
        + [pl.BlockSpec(memory_space=pl.ANY)] * len(prior),
        out_specs=[
            pl.BlockSpec((pixels, block), lambda i: (0, start + i)),
            pl.BlockSpec((pixels, block), lambda i: (0, start + i)),
            pl.BlockSpec((width, block), lambda i: (0, i)),
            pl.BlockSpec((width, block), lambda i: (0, i)),
            pl.BlockSpec((1, block), lambda i: (0, start + i)),
        ],
        out_shape=[whole, whole, grad, grad, jax.ShapeDtypeStruct((1, hidden), F32)],
        scratch_shapes=[pltpu.VMEM((width, pixels), BF16), pltpu.VMEM((width, pixels), BF16)],
        input_output_aliases={6 + n: k for n, k in enumerate((0, 1, 4)[: len(prior)])},
        cost_estimate=pl.CostEstimate(
            flops=8 * pixels * width * (last - first),
            transcendentals=2 * pixels * (last - first),
            bytes_accessed=4 * pixels * width + 8 * width * (last - first) + 4 * pixels * (last - first),
        ),
        name="mlp",
    )(core_side.reshape(1).astype(jnp.int32), normed, d_branch, w_one, b_one.reshape(1, -1), w_two, *prior)
    activated, d_up, keep, send, bias = results
    blocks = (width // SUBLANES, SUBLANES, last - first)
    return (activated, d_up, bias), (keep.reshape(blocks), send.reshape(blocks))


def norm_back_body(dup_ref, w_ref, conv_ref, norm_ref, dn_ref, part_ref):
    value = lax.dot_general(
        dup_ref[...], w_ref[...], (((1,), (1,)), ((), ())), preferred_element_type=F32
    )
    dn_ref[...] = value
    centered = (conv_ref[...] - norm_ref[0:1]) * norm_ref[1:2]

    @pl.when(pl.program_id(0) == 0)
    def _():
        part_ref[...] = jnp.zeros(part_ref.shape, F32)

    part_ref[0:1] += jnp.sum(value, axis=0, keepdims=True)
    part_ref[1:2] += jnp.sum(value * centered, axis=0, keepdims=True)


def norm_back(d_up, w_one, conv_flat, norm, row_block=256):
    pixels, hidden = d_up.shape
    width = w_one.shape[0]
    return pl.pallas_call(
        norm_back_body,
        grid=(pixels // row_block,),
        in_specs=[
            pl.BlockSpec((row_block, hidden), lambda i: (i, 0)),
            pl.BlockSpec((width, hidden), lambda i: (0, 0)),
            pl.BlockSpec((row_block, width), lambda i: (i, 0)),
            pl.BlockSpec((2, width), lambda i: (0, 0)),
        ],
        out_specs=[
            pl.BlockSpec((row_block, width), lambda i: (i, 0)),
            pl.BlockSpec((2, width), lambda i: (0, 0)),
        ],
        out_shape=[
            jax.ShapeDtypeStruct((pixels, width), F32),
            jax.ShapeDtypeStruct((2, width), F32),
        ],
        cost_estimate=pl.CostEstimate(
            flops=2 * pixels * width * hidden,
            transcendentals=0,
            bytes_accessed=2 * (pixels + width) * hidden + 8 * pixels * width,
        ),
        name="norm_back",
    )(d_up, w_one, conv_flat, norm)


def branch_out_body(act_ref, w_ref, b_ref, hidden_ref, wet_ref, w_out_ref, b_out_ref, dres_ref, result_ref, gout_ref):
    branch = b_ref[...] + lax.dot_general(
        act_ref[...], w_ref[...], (((1,), (1,)), ((), ())), preferred_element_type=F32
    )
    mixed = ((hidden_ref[...] + branch) * wet_ref[...]).astype(BF16)
    result = jnp.dot(mixed, w_out_ref[...], preferred_element_type=F32) + b_out_ref[...]
    result = result.T
    groups, count, padded_ch, lanes = result_ref.shape
    for row in range(count):
        for g in range(groups):
            piece = result[g * padded_ch : (g + 1) * padded_ch, row * lanes : (row + 1) * lanes]
            result_ref[g, row] = piece.astype(BF16)

    @pl.when(pl.program_id(0) == 0)
    def _():
        gout_ref[...] = jnp.zeros(gout_ref.shape, F32)

    gout_ref[...] += lax.dot_general(
        dres_ref[...], mixed, (((0,), (0,)), ((), ())), preferred_element_type=F32
    )


def branch_out(activated, w_two, b_two, hidden, wet, w_out_slots, b_slots, d_result, out_shape, row_block=256):
    pixels, inner = activated.shape
    width, slots = w_out_slots.shape
    return pl.pallas_call(
        branch_out_body,
        grid=(pixels // row_block,),
        in_specs=[
            pl.BlockSpec((row_block, inner), lambda i: (i, 0)),
            pl.BlockSpec((width, inner), lambda i: (0, 0)),
            pl.BlockSpec((1, width), lambda i: (0, 0)),
            pl.BlockSpec((row_block, width), lambda i: (i, 0)),
            pl.BlockSpec((row_block, 1), lambda i: (i, 0)),
            pl.BlockSpec((width, slots), lambda i: (0, 0)),
            pl.BlockSpec((1, slots), lambda i: (0, 0)),
            pl.BlockSpec((row_block, slots), lambda i: (i, 0)),
        ],
        out_specs=[
            pl.BlockSpec(
                (out_shape[0], row_block // out_shape[3]) + out_shape[2:], lambda i: (0, i, 0, 0)
            ),
            pl.BlockSpec((slots, width), lambda i: (0, 0)),
        ],
        out_shape=[
            jax.ShapeDtypeStruct(out_shape, BF16),
            jax.ShapeDtypeStruct((slots, width), F32),
        ],
        cost_estimate=pl.CostEstimate(
            flops=2 * pixels * width * (inner + 2 * slots),
            transcendentals=0,
            bytes_accessed=2 * (pixels + width) * inner + 4 * pixels * width,
        ),
        name="branch_out",
    )(activated, w_two, b_two.reshape(1, -1), hidden, wet, w_out_slots, b_slots.reshape(1, -1), d_result)


def conv_back_body(rows, cols, half, edge_ref, coef_ref, dn_ref, conv_ref, dsum_ref, low_ref, depth_ref, dh_ref, dh_low_ref, dh_high_ref, gw_ref, gb_ref, dc_ref, dl_ref, pad_ref, tap_ref):
    kernel = 2 * half + 1
    wide = cols + 2 * half
    d_conv = coef_ref[0:1] * dn_ref[...] + (coef_ref[1:2] * conv_ref[...] + coef_ref[2:3])
    dc_ref[...] = d_conv.astype(BF16).astype(F32)
    dl_ref[...] = jnp.zeros(dl_ref.shape, F32)
    dl_ref[half : half + rows, half : half + cols] = dsum_ref[...]
    pad_ref[...] = low_ref[...].astype(F32).reshape(pad_ref.shape)
    tap_ref[...] = jnp.zeros(tap_ref.shape, F32)

    def one_row(row, carry):
        source = [dc_ref[row, c] for c in range(cols)]
        for i in range(kernel):
            taps = [jnp.broadcast_to(depth_ref[i * kernel + j], (SUBLANES, LANES)) for j in range(kernel)]
            for c in range(wide):
                acc = dl_ref[row + i, c]
                for j in range(kernel):
                    if 0 <= c - j < cols:
                        acc = acc + source[c - j] * taps[j]
                dl_ref[row + i, c] = acc
        for i in range(kernel):
            sums = [tap_ref[i * kernel + j] for j in range(kernel)]
            for c in range(wide):
                value = pad_ref[row + i, c]
                for j in range(kernel):
                    if 0 <= c - j < cols:
                        sums[j] = sums[j] + source[c - j] * value
            for j in range(kernel):
                tap_ref[i * kernel + j] = sums[j]
        return carry

    lax.fori_loop(0, rows, one_row, 0)

    @pl.when(edge_ref[0] == 1)
    def _():
        dl_ref[:half] = jnp.zeros((half,) + dl_ref.shape[1:], F32)

    @pl.when(edge_ref[1] == 1)
    def _():
        dl_ref[half + rows :] = jnp.zeros((half,) + dl_ref.shape[1:], F32)

    @pl.when(edge_ref[2] == 1)
    def _():
        dl_ref[:, :half] = jnp.zeros((dl_ref.shape[0], half) + dl_ref.shape[2:], F32)

    @pl.when(edge_ref[3] == 1)
    def _():
        dl_ref[:, half + cols :] = jnp.zeros((dl_ref.shape[0], half) + dl_ref.shape[2:], F32)

    d_hidden = dl_ref[...]
    dh_ref[...] = d_hidden[:, half : half + cols].reshape(dh_ref.shape).astype(BF16)
    dh_low_ref[...] = d_hidden[:, :half].reshape(dh_low_ref.shape).astype(BF16)
    dh_high_ref[...] = d_hidden[:, half + cols :].reshape(dh_high_ref.shape).astype(BF16)
    gb_ref[...] = jnp.sum(jnp.sum(d_hidden, axis=(0, 1)), axis=0, keepdims=True)
    gw_ref[...] = jnp.sum(tap_ref[...], axis=1)


def conv_back(edges, coef, d_normed, conv_out, d_sum, lowered, depth, tile, first, last, prior=()):
    rows, cols, dates, half = tile
    taps = depth.shape[0]
    width = lowered.shape[1]
    padded = lowered.shape[0]
    inner = pl.BlockSpec((rows, cols, dates, LANES), lambda i: (0, 0, 0, first + i))
    wide = (rows + 2 * half, cols + 2 * half, dates, LANES)
    inside = (rows + 2 * half) * cols * dates
    beside = (rows + 2 * half) * half * dates

    def body(edge_ref, coef_ref, dn_ref, conv_ref, dsum_ref, low_ref, depth_ref, *refs):
        conv_back_body(rows, cols, half, edge_ref, coef_ref, dn_ref, conv_ref, dsum_ref, low_ref, depth_ref, *refs[len(prior) :])

    return pl.pallas_call(
        body,
        grid=(last - first,),
        in_specs=[
            pl.BlockSpec(memory_space=pltpu.SMEM),
            pl.BlockSpec((3, LANES), lambda i: (0, first + i)),
            inner,
            inner,
            inner,
            pl.BlockSpec((padded, LANES), lambda i: (0, first + i)),
            pl.BlockSpec((taps, 1, LANES), lambda i: (0, 0, first + i)),
        ]
        + [pl.BlockSpec(memory_space=pl.ANY)] * len(prior),
        out_specs=[
            pl.BlockSpec((count, LANES), lambda i: (0, first + i)) for count in (inside, beside, beside, taps, 1)
        ],
        out_shape=[
            jax.ShapeDtypeStruct((inside, width), BF16),
            jax.ShapeDtypeStruct((beside, width), BF16),
            jax.ShapeDtypeStruct((beside, width), BF16),
            jax.ShapeDtypeStruct((taps, width), F32),
            jax.ShapeDtypeStruct((1, width), F32),
        ],
        scratch_shapes=[
            pltpu.VMEM((rows, cols, dates, LANES), F32),
            pltpu.VMEM(wide, F32),
            pltpu.VMEM(wide, F32),
            pltpu.VMEM((taps, dates, LANES), F32),
        ],
        input_output_aliases={7 + k: k for k in range(len(prior))},
        cost_estimate=pl.CostEstimate(
            flops=4000000000 * (last - first),
            transcendentals=0,
            bytes_accessed=16 * padded * LANES * (last - first),
        ),
        name="conv_back",
    )(edges, coef, d_normed, conv_out, d_sum, lowered, depth, *prior)


def input_back(dh, dh_low, dh_high, x, x_low, x_high, w_slots, row_block=256):
    slots, width = w_slots.shape
    inside, beside = dh.shape[0], dh_low.shape[0]
    mix = (((1,), (1,)), ((), ()))
    down = (((0,), (0,)), ((), ()))

    def body(dh_ref, dl_ref, dr_ref, x_ref, xl_ref, xr_ref, w_ref, ds_ref, sl_ref, sr_ref, g_ref):
        ds_ref[...] = lax.dot_general(dh_ref[...], w_ref[...], mix, preferred_element_type=F32)

        @pl.when(pl.program_id(0) == 0)
        def _():
            sl_ref[...] = lax.dot_general(
                dl_ref[...], w_ref[...], mix, preferred_element_type=F32
            ).astype(BF16)
            sr_ref[...] = lax.dot_general(
                dr_ref[...], w_ref[...], mix, preferred_element_type=F32
            ).astype(BF16)
            g_ref[...] = lax.dot_general(
                xl_ref[...], dl_ref[...], down, preferred_element_type=F32
            ) + lax.dot_general(xr_ref[...], dr_ref[...], down, preferred_element_type=F32)

        g_ref[...] += lax.dot_general(x_ref[...], dh_ref[...], down, preferred_element_type=F32)

    moving = lambda i: (i, 0)
    fixed = lambda i: (0, 0)
    return pl.pallas_call(
        body,
        grid=(inside // row_block,),
        in_specs=[
            pl.BlockSpec((row_block, width), moving),
            pl.BlockSpec((beside, width), fixed),
            pl.BlockSpec((beside, width), fixed),
            pl.BlockSpec((row_block, slots), moving),
            pl.BlockSpec((beside, slots), fixed),
            pl.BlockSpec((beside, slots), fixed),
            pl.BlockSpec((slots, width), fixed),
        ],
        out_specs=[
            pl.BlockSpec((row_block, slots), moving),
            pl.BlockSpec((beside, slots), fixed),
            pl.BlockSpec((beside, slots), fixed),
            pl.BlockSpec((slots, width), fixed),
        ],
        out_shape=[
            jax.ShapeDtypeStruct((inside, slots), F32),
            jax.ShapeDtypeStruct((beside, slots), BF16),
            jax.ShapeDtypeStruct((beside, slots), BF16),
            jax.ShapeDtypeStruct((slots, width), F32),
        ],
        name="input_back",
    )(dh, dh_low, dh_high, x, x_low, x_high, w_slots)


def to_groups(d_state, from_high, from_low, groups):
    rows, pixels, slots = d_state.shape
    beside = from_low.shape[1]
    padded_ch = slots // groups

    def body(in_ref, high_ref, low_ref, out_ref):
        for row in range(rows):
            value = in_ref[row]
            first = value[:beside] + low_ref[row].astype(F32)
            last = value[pixels - beside :] + high_ref[row].astype(F32)
            value = jnp.concatenate([first, value[beside : pixels - beside], last], axis=0).T
            for g in range(groups):
                out_ref[g, row] = value[g * padded_ch : (g + 1) * padded_ch].astype(BF16)

    return pl.pallas_call(
        body,
        out_shape=jax.ShapeDtypeStruct((groups, rows, padded_ch, pixels), BF16),
        name="to_groups",
    )(d_state, from_high, from_low)


def on_device(
    ocean_state,
    slot_level,
    wet_mask,
    w_in,
    b_in,
    w_depth,
    norm_gain,
    norm_bias,
    w_one,
    b_one,
    w_two,
    b_two,
    w_out,
    b_out,
    cotangent,
):
    groups = lax.axis_size("lev")
    strips = lax.axis_size("sp")
    group_index = lax.axis_index("lev")
    strip_index = lax.axis_index("sp")
    rows, cols = wet_mask.shape
    all_rows, dates, _, group_ch = ocean_state.shape
    padded_ch = -(-group_ch // SUBLANES) * SUBLANES
    slots = padded_ch * groups
    channels, width = w_in.shape
    kernel = w_depth.shape[0]
    half = kernel // 2
    tile = (rows, cols, dates, half)
    high_rows = rows + 2 * half
    pixels = rows * cols * dates
    pixel_total = float(pixels * groups * strips)

    lev_stages = bits_of("lev")
    sp_stages = bits_of("sp")
    stages = lev_stages + sp_stages
    core, lev_rest = lev_stages[:1], lev_stages[1:]
    orders = (
        core + lev_rest + sp_stages,
        core + sp_stages[:1] + lev_rest + sp_stages[1:],
        core + sp_stages[1:2] + lev_rest + sp_stages[:1] + sp_stages[2:],
    )
    forward = [(i, i + 1) for i in range(strips - 1)]
    backward = [(i + 1, i) for i in range(strips - 1)]
    edges = jnp.stack(
        [group_index == 0, group_index == groups - 1, strip_index == 0, strip_index == strips - 1]
    ).astype(jnp.int32)

    table = slot_table(slot_level, groups, group_ch, padded_ch, channels)
    table_low = table.astype(BF16)
    w_slots = jnp.dot(table_low, w_in, preferred_element_type=F32).astype(BF16)
    w_out_slots = jnp.dot(w_out, table_low.T, preferred_element_type=F32).astype(BF16)
    b_slots = jnp.dot(table, b_out, precision=exact_mode)
    depth = w_depth.astype(F32).reshape(kernel * kernel, 1, width)

    row_pixels = cols * dates
    beside = half * dates
    windows, d_result = to_channel_rows(ocean_state, cotangent, groups, half, padded_ch)
    windows = lax.all_to_all(windows, "lev", split_axis=0, concat_axis=0, tiled=True)
    d_result = lax.all_to_all(
        after(d_result, windows), "lev", split_axis=0, concat_axis=0, tiled=True
    )
    x_rows = to_pixel_rows(windows)
    x_low = lax.ppermute(x_rows[:, row_pixels - beside :], "sp", forward).reshape(-1, slots)
    x_high = lax.ppermute(x_rows[:, :beside], "sp", backward).reshape(-1, slots)
    x_rows = x_rows.reshape(-1, slots)
    d_result = to_pixel_rows(d_result).reshape(pixels, slots)

    hidden, lowered, conv_out, local = hidden_conv(
        edges, x_rows, x_low, x_high, w_slots, b_in, depth, tile
    )
    total = butterfly(local, stages)
    wet = jnp.broadcast_to(
        wet_mask.astype(F32)[:, :, None, None], (rows, cols, dates, 1)
    ).reshape(pixels, 1)
    d_mixed = jnp.dot(d_result, w_out_slots.T, preferred_element_type=F32)
    d_sum = d_mixed * wet
    d_branch = d_sum.astype(BF16)
    g_b_two = jnp.sum(d_branch.astype(F32), axis=0)
    g_bias_slots = jnp.sum(d_result.astype(F32), axis=0)

    mean_value = total[0] / pixel_total
    inv_scale = lax.rsqrt(total[1] / pixel_total - mean_value * mean_value + 1e-05)
    conv_flat = conv_out.reshape(pixels, width)
    centered = (conv_flat - mean_value) * inv_scale
    normed = (centered * norm_gain + norm_bias).astype(BF16)
    ff = w_one.shape[1]
    block = 256
    cuts = [0, 2 * ff // 5 // block * block, 4 * ff // 5 // block * block, ff]
    flight = Exchanges()

    def as_rows(vector):
        flat = vector.reshape(-1)
        count = -(-flat.shape[0] // width)
        return jnp.pad(flat, (0, count * width - flat.shape[0])).reshape(count, width)

    w_two_t = w_two.T
    core_side = side(core[0])

    def part(number, prior=()):
        return mlp(
            core_side, normed, d_branch, w_one, b_one, w_two_t, cuts[number], cuts[number + 1], prior
        )

    def begin(name, grads, order):
        return flight.begin(name, grads[0], order, BF16, partner=grads[1])

    found, grads = part(0)
    sent = begin("a", grads, orders[0])
    found, grads = part(1, (after(found[0], sent),) + found[1:])
    sent = flight.step(found[2], "a")
    sent.append(begin("b", grads, orders[1]))
    found, grads = part(2, (after(found[0], *sent),) + found[1:])
    sent = flight.step(found[2], "b")
    sent.append(begin("c", grads, orders[2]))
    activated, d_up, g_b_one = found

    norm = jnp.stack([mean_value, inv_scale])
    d_normed, parts = norm_back(after(d_up, *sent), w_one, conv_flat, norm)
    sent = flight.step(parts, "a", "c")
    parts = jnp.concatenate(
        [parts, as_rows(g_b_one), as_rows(g_b_two), as_rows(g_bias_slots)], axis=0
    )
    first_hop = hop(parts, stages[0])
    result, g_out_slots = branch_out(
        after(activated, parts, *sent),
        w_two_t,
        b_two,
        hidden.reshape(pixels, width),
        wet,
        w_out_slots,
        b_slots,
        d_result,
        (groups, rows, padded_ch, row_pixels),
    )
    sent = flight.step(g_out_slots, "a", "b", "c")
    parts, *_ = lax.optimization_barrier((parts, *sent))
    summed = butterfly(parts + after(first_hop, g_out_slots), stages[1:])
    norm_grads = summed[:2]
    sent = flight.step(summed, "a", "b", "c")

    next_state = lax.all_to_all(result, "lev", split_axis=0, concat_axis=0, tiled=True)
    next_state = from_channel_rows(next_state, 0, dates, cols, group_ch)

    scale = norm_gain * inv_scale
    slope = scale * inv_scale * (norm_grads[1] / pixel_total)
    coef = jnp.stack(
        [scale, -slope, slope * mean_value - scale * (norm_grads[0] / pixel_total)]
    )
    shape4 = (rows, cols, dates, width)
    inputs = (d_normed.reshape(shape4), conv_out, d_sum.reshape(shape4), lowered, depth, tile)
    tiles = pl.cdiv(width, LANES)
    steps = [0, 2, 4, tiles]
    moves = (("a", "b", "c"),) * 3
    found = ()
    for first, last, names in zip(steps[:-1], steps[1:], moves):
        found = conv_back(edges, after(coef, *sent), *inputs, first, last, found)
        sent = flight.step(found[4], *names)
    d_hidden, d_low, d_high, g_w_depth, g_b_in = found
    d_state, d_low, d_high, g_in_slots = input_back(
        after(d_hidden, *sent), d_low, d_high, x_rows, x_low, x_high, w_slots
    )
    from_high = lax.ppermute(d_low.reshape(high_rows, beside, slots), "sp", backward)
    from_low = lax.ppermute(d_high.reshape(high_rows, beside, slots), "sp", forward)
    d_state = to_groups(
        d_state.reshape(high_rows, row_pixels, slots), from_high, from_low, groups
    )
    d_state = lax.all_to_all(d_state, "lev", split_axis=0, concat_axis=0, tiled=True)
    grad_ocean_state = from_channel_rows(d_state, half, dates, cols, group_ch)

    def pack(arrays):
        packed = jnp.concatenate(arrays, axis=0)
        return jnp.pad(packed, ((0, -packed.shape[0] % (16 * SUBLANES)), (0, 0))).reshape(
            -1, SUBLANES, width
        )

    def unpack(packed, arrays):
        packed = packed.reshape(-1, width)
        found = []
        start = 0
        for array in arrays:
            found.append(packed[start : start + array.shape[0]])
            start += array.shape[0]
        return found

    last_sums = [g_out_slots, g_in_slots, g_w_depth, g_b_in]
    flight.begin("small", pack(last_sums), orders[0], BF16, most=3)
    flight.finish(g_b_in, "small", "a", "b", "c")
    g_out_slots, g_in_slots, g_w_depth, g_b_in = unpack(in_order(*flight.done["small"]), last_sums)
    weights = ()
    for name, start in zip("acb", (cuts[0], cuts[2], cuts[1])):
        weights = unpack_grads(core_side, flight.done[name], width, ff, start, weights)
    grad_w_one, grad_w_two = weights
    grad_w_out = jnp.einsum("sd,sc->dc", g_out_slots.astype(F32), table, precision=exact_mode)
    count = -(-ff // width)
    grad_b_one = summed[2 : 2 + count].reshape(-1)[:ff]
    grad_b_two = summed[2 + count]
    grad_b_out = jnp.dot(summed[3 + count, :slots], table, precision=exact_mode)
    grad_w_in = jnp.dot(table.T, g_in_slots.astype(F32), precision=exact_mode)
    grad_w_depth = g_w_depth.astype(F32).reshape(kernel, kernel, width)
    grad_b_in = g_b_in.astype(F32).reshape(-1)
    return (
        next_state,
        grad_ocean_state,
        grad_w_in,
        grad_b_in,
        grad_w_depth,
        norm_grads[1],
        norm_grads[0],
        grad_w_one,
        grad_b_one,
        grad_w_two.T,
        grad_b_two,
        grad_w_out,
        grad_b_out,
    )


def solution(mesh):
    return jax.shard_map(
        on_device,
        mesh=mesh,
        in_specs=(
            P(None, None, "sp", "lev"),
            P(),
            P("lev", "sp"),
            P(),
            P(),
            P(),
            P(),
            P(),
            P(),
            P(),
            P(),
            P(),
            P(),
            P(),
            P(None, None, "sp", "lev"),
        ),
        out_specs=(
            P(None, None, "sp", "lev"),
            P(None, None, "sp", "lev"),
            P(),
            P(),
            P(),
            P(),
            P(),
            P(),
            P(),
            P(),
            P(),
            P(),
            P(),
        ),
        check_vma=False,
    )
```

```python
import functools

import jax
import jax.numpy as jnp
from jax import lax
from jax.experimental import pallas as pl
from jax.experimental.pallas import tpu as pltpu
from jax.sharding import PartitionSpec as P

VARS = 10
LANES = 128
SUBLANES = 8

exact_mode = lax.Precision.HIGHEST
F32 = jnp.float32
BF16 = jnp.bfloat16

COST = pl.CostEstimate(flops=50000000000, transcendentals=0, bytes_accessed=50000000)

TAIL_SCALE = 0.3
TAIL_POLY = (
    0.119623263,
    0.120845528,
    0.0993471402,
    0.130416391,
    -0.0571672287,
    0.210118226,
    -0.159378204,
    0.0361948279,
)


def slot_table(levels_of_slots, groups, group_ch, padded_ch, channels):
    slot_count = groups * group_ch
    kinds = jnp.arange(slot_count) % VARS
    target = jnp.repeat(levels_of_slots, VARS) * VARS + kinds
    target = jnp.pad(
        target.reshape(groups, group_ch), ((0, 0), (0, padded_ch - group_ch)), constant_values=-1
    ).reshape(-1)
    columns = jnp.arange(channels)
    return (target[:, None] == columns[None, :]).astype(F32)


def bits_of(axis):
    size = lax.axis_size(axis)
    return [(axis, 1 << k) for k in range(size.bit_length() - 1)]


def hop(value, stage):
    axis, bit = stage
    return lax.ppermute(value, axis, [(i, i ^ bit) for i in range(lax.axis_size(axis))])


def side(stage):
    axis, bit = stage
    return (lax.axis_index(axis) // bit) % 2


def butterfly(value, stages):
    for stage in stages:
        value = value + hop(value, stage)
    return value


def after(value, *earlier):
    return lax.optimization_barrier((value,) + earlier)[0]


def halves(value, axis, bit):
    half = value.shape[axis] // 2
    stay = lax.dynamic_slice_in_dim(value, bit * half, half, axis)
    sent = lax.dynamic_slice_in_dim(value, (1 - bit) * half, half, axis)
    return stay, sent


def halving_lanes(lanes):
    tiles = lanes // LANES
    return lanes % LANES == 0 and (tiles % 2 == 0 or tiles >= 9)


def total(terms):
    value = terms[0].astype(F32)
    for term in terms[1:]:
        value = value + term.astype(F32)
    return value


def exchange(value, stages, link, partner=None, most=2):
    kept = []
    own = 0
    lanes = value.shape[2]
    terms = [value]
    rest = stages
    if partner is not None:
        came = hop(partner, stages[0])
        token = yield partner
        terms.append(after(came, token))
        rest = stages[1:]
    row_halvings = 0
    for stage in rest:
        bit = side(stage)
        shape = terms[0].shape
        if stage is rest[-1]:
            axis = None
        elif shape[0] % 2 == 0 and row_halvings < most:
            axis = 0
            row_halvings += 1
            own = own * 2 + bit
        else:
            axis = 2 if halving_lanes(shape[2]) else None
        if axis is None:
            sent = total(terms).astype(link)
            terms = [sent]
        else:
            if axis == 2 and shape[2] // LANES % 2:
                terms = [jnp.pad(term, ((0, 0), (0, 0), (0, LANES))) for term in terms]
            pairs = [halves(term, axis, bit) for term in terms]
            sent = total([pair[1] for pair in pairs]).astype(link)
            terms = [pair[0] for pair in pairs]
            kept.append((stage, axis))
        came = hop(sent, stage)
        token = yield sent
        terms.append(after(came, token))
    value = total(terms).astype(link)
    for stage, axis in reversed(kept):
        came = hop(value, stage)
        token = yield value
        came = after(came, token)
        if axis == 0:
            value = jnp.concatenate([value, came], axis=0)
        else:
            bit = side(stage)
            low = jnp.where(bit == 0, value, came)
            high = jnp.where(bit == 0, came, value)
            value = jnp.concatenate([low, high], axis=2)[:, :, :lanes]
    other = None
    if partner is not None:
        came = hop(value, stages[0])
        token = yield value
        other = after(came, token)
    yield value, other, own, 1 << row_halvings


def in_order(value, other, own, pieces):
    count = value.shape[0] // pieces
    return jnp.concatenate(
        [lax.dynamic_slice_in_dim(value, (index ^ own) * count, count, 0) for index in range(pieces)],
        axis=0,
    )


class Exchanges:
    def __init__(self):
        self.running = {}
        self.done = {}

    def begin(self, name, *args, **options):
        self.running[name] = exchange(*args, **options)
        return next(self.running[name])

    def step(self, token, *names):
        sent = []
        for name in names:
            if name in self.running:
                got = self.running[name].send(token)
                if isinstance(got, tuple):
                    self.done[name] = got
                    del self.running[name]
                else:
                    sent.append(got)
        return sent

    def finish(self, token, *names):
        while any(name in self.running for name in names):
            self.step(token, *names)


def unpack_grads(core_side, reduced, width, ff, start, prior=()):
    value, other, own, pieces = reduced
    count = value.shape[0] // pieces
    rows = count * SUBLANES
    columns = value.shape[2]

    def body(own_ref, value_ref, other_ref, *refs):
        out_one, out_two = refs[len(prior) :]
        mine = value_ref[...].astype(F32).reshape(rows, columns)
        theirs = other_ref[...].astype(F32).reshape(rows, columns)
        first = own_ref[1] == 0

        @pl.when(first)
        def _():
            out_one[...] = mine
            out_two[...] = theirs

        @pl.when(jnp.logical_not(first))
        def _():
            out_one[...] = theirs
            out_two[...] = mine

    out = pl.BlockSpec((pl.Element(rows), pl.Element(columns)), lambda i, own: (i * rows, start))
    piece = pl.BlockSpec((count, SUBLANES, columns), lambda i, own: (i ^ own[0], 0, 0))
    return pl.pallas_call(
        body,
        grid_spec=pltpu.PrefetchScalarGridSpec(
            num_scalar_prefetch=1,
            grid=(pieces,),
            in_specs=[piece, piece] + [pl.BlockSpec(memory_space=pl.ANY)] * len(prior),
            out_specs=[out, out],
        ),
        out_shape=[jax.ShapeDtypeStruct((width, ff), F32)] * 2,
        input_output_aliases={3 + k: k for k in range(len(prior))},
        cost_estimate=COST,
        name="unpack_grads",
    )(jnp.stack([own, core_side]).astype(jnp.int32), value, other, *prior)


def pixel_order(dates, cols):
    pixels = dates * cols
    source = lax.broadcasted_iota(jnp.int32, (pixels, pixels), 0)
    place = lax.broadcasted_iota(jnp.int32, (pixels, pixels), 1)
    return ((source % cols) * dates + source // cols == place).astype(BF16)


def to_channel_rows(state, cotangent, groups, half, padded_ch):
    all_rows, dates, cols, ch = state.shape
    rows = all_rows // groups
    high = rows + 2 * half
    pixels = dates * cols

    def body(state_ref, cot_ref, window_ref, ct_ref):
        perm = pixel_order(dates, cols)
        blank = jnp.zeros((padded_ch - ch, pixels), F32)
        zero = jnp.zeros((padded_ch, pixels), BF16)

        def turned(ref, row):
            value = lax.dot_general(
                ref[row].reshape(pixels, ch), perm, (((0,), (0,)), ((), ())), preferred_element_type=F32
            )
            return jnp.concatenate([value, blank], axis=0).astype(BF16) if padded_ch > ch else value.astype(BF16)

        for row in range(half):
            window_ref[0, row] = zero
            window_ref[groups - 1, half + rows + row] = zero
        for row in range(all_rows):
            value = turned(state_ref, row)
            for band in range(groups):
                place = row - band * rows + half
                if 0 <= place < high:
                    window_ref[band, place] = value
            ct_ref[row // rows, row % rows] = turned(cot_ref, row)

    return pl.pallas_call(
        body,
        out_shape=[
            jax.ShapeDtypeStruct((groups, high, padded_ch, pixels), BF16),
            jax.ShapeDtypeStruct((groups, rows, padded_ch, pixels), BF16),
        ],
        cost_estimate=COST,
        name="to_channel_rows",
    )(state, cotangent)


def from_channel_rows(windows, half, dates, cols, ch):
    groups, high, padded_ch, pixels = windows.shape
    rows = high - 2 * half

    def body(window_ref, out_ref):
        perm = pixel_order(dates, cols)
        for row in range(groups * rows):
            value = None
            for band in range(groups):
                place = row - band * rows + half
                if 0 <= place < high:
                    piece = window_ref[band, place]
                    value = piece if value is None else value.astype(F32) + piece.astype(F32)
            value = lax.dot_general(
                perm, value.astype(BF16), (((1,), (1,)), ((), ())), preferred_element_type=F32
            )
            out_ref[row] = value[:, :ch].astype(BF16).reshape(dates, cols, ch)

    return pl.pallas_call(
        body,
        out_shape=jax.ShapeDtypeStruct((groups * rows, dates, cols, ch), BF16),
        cost_estimate=COST,
        name="from_channel_rows",
    )(windows)


def to_pixel_rows(received):
    groups, rows, padded_ch, pixels = received.shape
    slots = groups * padded_ch

    def body(in_ref, out_ref):
        for row in range(rows):
            value = jnp.concatenate([in_ref[g, row].astype(F32) for g in range(groups)], axis=0)
            out_ref[row] = value.T.astype(BF16)

    return pl.pallas_call(
        body,
        out_shape=jax.ShapeDtypeStruct((rows, pixels, slots), BF16),
        cost_estimate=COST,
        name="to_pixel_rows",
    )(received)


def hidden_conv_body(rows, cols, half, edge_ref, x_ref, low_x_ref, high_x_ref, w_ref, b_ref, depth_ref, hidden_ref, low_ref, conv_ref, stat_ref, pad_ref):
    kernel = 2 * half + 1
    high = rows + 2 * half

    def hidden_of(ref, columns):
        value = jnp.dot(ref[...], w_ref[...], preferred_element_type=F32) + b_ref[...]
        return value.reshape(high, columns, SUBLANES, LANES)

    value = hidden_of(x_ref, cols)
    hidden_ref[...] = value[half : half + rows]
    pad_ref[:, half : half + cols] = value.astype(BF16).astype(F32)
    pad_ref[:, :half] = hidden_of(low_x_ref, half).astype(BF16).astype(F32)
    pad_ref[:, half + cols :] = hidden_of(high_x_ref, half).astype(BF16).astype(F32)

    @pl.when(edge_ref[0] == 1)
    def _():
        pad_ref[:half] = jnp.zeros((half,) + pad_ref.shape[1:], F32)

    @pl.when(edge_ref[1] == 1)
    def _():
        pad_ref[half + rows :] = jnp.zeros((half,) + pad_ref.shape[1:], F32)

    @pl.when(edge_ref[2] == 1)
    def _():
        pad_ref[:, :half] = jnp.zeros((pad_ref.shape[0], half) + pad_ref.shape[2:], F32)

    @pl.when(edge_ref[3] == 1)
    def _():
        pad_ref[:, half + cols :] = jnp.zeros((pad_ref.shape[0], half) + pad_ref.shape[2:], F32)

    low_ref[...] = pad_ref[...].reshape(low_ref.shape).astype(BF16)

    def one_row(row, carry):
        total, square = carry
        acc = jnp.zeros((cols, SUBLANES, LANES), F32)
        for i in range(kernel):
            slab = pad_ref[row + i]
            for j in range(kernel):
                acc = acc + slab[j : j + cols] * depth_ref[i * kernel + j]
        conv_ref[row] = acc
        return total + jnp.sum(acc, axis=0), square + jnp.sum(acc * acc, axis=0)

    zero = jnp.zeros((SUBLANES, LANES), F32)
    total, square = lax.fori_loop(0, rows, one_row, (zero, zero))
    stat_ref[0:1] = jnp.sum(total, axis=0, keepdims=True)
    stat_ref[1:2] = jnp.sum(square, axis=0, keepdims=True)


def hidden_conv(edges, x, low_x, high_x, w_slots, b_in, depth, tile):
    rows, cols, dates, half = tile
    slots, width = w_slots.shape
    padded = (rows + 2 * half) * (cols + 2 * half) * dates
    return pl.pallas_call(
        functools.partial(hidden_conv_body, rows, cols, half),
        grid=(pl.cdiv(width, LANES),),
        in_specs=[
            pl.BlockSpec(memory_space=pltpu.SMEM),
            pl.BlockSpec(x.shape, lambda i: (0, 0)),
            pl.BlockSpec(low_x.shape, lambda i: (0, 0)),
            pl.BlockSpec(high_x.shape, lambda i: (0, 0)),
            pl.BlockSpec((slots, LANES), lambda i: (0, i)),
            pl.BlockSpec((1, LANES), lambda i: (0, i)),
            pl.BlockSpec((depth.shape[0], 1, LANES), lambda i: (0, 0, i)),
        ],
        out_specs=[
            pl.BlockSpec((rows, cols, dates, LANES), lambda i: (0, 0, 0, i)),
            pl.BlockSpec((padded, LANES), lambda i: (0, i)),
            pl.BlockSpec((rows, cols, dates, LANES), lambda i: (0, 0, 0, i)),
            pl.BlockSpec((2, LANES), lambda i: (0, i)),
        ],
        out_shape=[
            jax.ShapeDtypeStruct((rows, cols, dates, width), F32),
            jax.ShapeDtypeStruct((padded, width), BF16),
            jax.ShapeDtypeStruct((rows, cols, dates, width), F32),
            jax.ShapeDtypeStruct((2, width), F32),
        ],
        scratch_shapes=[pltpu.VMEM((rows + 2 * half, cols + 2 * half, dates, LANES), F32)],

        cost_estimate=COST,
        name="hidden_conv",
    )(edges, x, low_x, high_x, w_slots, b_in.reshape(1, -1), depth)


def gelu_pair(values):
    size = jnp.abs(values)
    gauss = jnp.exp(-0.5 * values * values)
    t = 1.0 / (1.0 + TAIL_SCALE * size)
    poly = jnp.full_like(t, TAIL_POLY[-1])
    for factor in TAIL_POLY[-2::-1]:
        poly = poly * t + factor
    tail = gauss * (t * poly)
    below = jnp.where(values >= 0, 1.0 - tail, tail)
    return values * below, below + values * (gauss * 0.3989422804014327)


def mlp_body(row_block, core_ref, normed_ref, branch_ref, w_one_ref, b_one_ref, w_two_ref, act_ref, dup_ref, keep_ref, send_ref, gb_ref, normed_t, branch_t):
    @pl.when(pl.program_id(0) == 0)
    def _():
        normed_t[...] = normed_ref[...].T
        branch_t[...] = branch_ref[...].T

    total = jnp.zeros((1, act_ref.shape[1]), F32)
    for start in range(0, normed_ref.shape[0], row_block):
        rows = pl.ds(start, row_block)
        up = jnp.dot(normed_ref[rows], w_one_ref[...], preferred_element_type=F32) + b_one_ref[...]
        d_act = jnp.dot(branch_ref[rows], w_two_ref[...], preferred_element_type=F32)
        value, slope = gelu_pair(up)
        act_ref[rows] = value.astype(BF16)
        d_up = (slope * d_act).astype(BF16)
        dup_ref[rows] = d_up
        total = total + jnp.sum(d_up.astype(F32), axis=0, keepdims=True)
    gb_ref[...] = total
    grad_one = jnp.dot(normed_t[...], dup_ref[...], preferred_element_type=F32).astype(BF16)
    grad_two = jnp.dot(branch_t[...], act_ref[...], preferred_element_type=F32).astype(BF16)
    first = core_ref[0] == 0

    @pl.when(first)
    def _():
        keep_ref[...] = grad_one
        send_ref[...] = grad_two

    @pl.when(jnp.logical_not(first))
    def _():
        keep_ref[...] = grad_two
        send_ref[...] = grad_one


def mlp(core_side, normed, d_branch, w_one, b_one, w_two, first, last, prior=(), block=256, row_block=128):
    pixels, width = normed.shape
    hidden = w_one.shape[1]
    start = first // block

    def body(core_ref, normed_ref, branch_ref, w_one_ref, b_one_ref, w_two_ref, *refs):
        mlp_body(row_block, core_ref, normed_ref, branch_ref, w_one_ref, b_one_ref, w_two_ref, *refs[len(prior) :])

    whole = jax.ShapeDtypeStruct((pixels, hidden), BF16)
    grad = jax.ShapeDtypeStruct((width, last - first), BF16)
    results = pl.pallas_call(
        body,
        grid=(pl.cdiv(last - first, block),),
        in_specs=[
            pl.BlockSpec(memory_space=pltpu.SMEM),
            pl.BlockSpec((pixels, width), lambda i: (0, 0)),
            pl.BlockSpec((pixels, width), lambda i: (0, 0)),
            pl.BlockSpec((width, block), lambda i: (0, start + i)),
            pl.BlockSpec((1, block), lambda i: (0, start + i)),
            pl.BlockSpec((width, block), lambda i: (0, start + i)),
        ]
        + [pl.BlockSpec(memory_space=pl.ANY)] * len(prior),
        out_specs=[
            pl.BlockSpec((pixels, block), lambda i: (0, start + i)),
            pl.BlockSpec((pixels, block), lambda i: (0, start + i)),
            pl.BlockSpec((width, block), lambda i: (0, i)),
            pl.BlockSpec((width, block), lambda i: (0, i)),
            pl.BlockSpec((1, block), lambda i: (0, start + i)),
        ],
        out_shape=[whole, whole, grad, grad, jax.ShapeDtypeStruct((1, hidden), F32)],
        scratch_shapes=[pltpu.VMEM((width, pixels), BF16), pltpu.VMEM((width, pixels), BF16)],
        input_output_aliases={6 + n: k for n, k in enumerate((0, 1, 4)[: len(prior)])},

        cost_estimate=COST,
        name="mlp",
    )(core_side.reshape(1).astype(jnp.int32), normed, d_branch, w_one, b_one.reshape(1, -1), w_two, *prior)
    activated, d_up, keep, send, bias = results
    blocks = (width // SUBLANES, SUBLANES, last - first)
    return (activated, d_up, bias), (keep.reshape(blocks), send.reshape(blocks))


def norm_back_body(dup_ref, w_ref, conv_ref, norm_ref, dn_ref, part_ref):
    value = lax.dot_general(
        dup_ref[...], w_ref[...], (((1,), (1,)), ((), ())), preferred_element_type=F32
    )
    dn_ref[...] = value
    centered = (conv_ref[...] - norm_ref[0:1]) * norm_ref[1:2]

    @pl.when(pl.program_id(0) == 0)
    def _():
        part_ref[...] = jnp.zeros(part_ref.shape, F32)

    part_ref[0:1] += jnp.sum(value, axis=0, keepdims=True)
    part_ref[1:2] += jnp.sum(value * centered, axis=0, keepdims=True)


def norm_back(d_up, w_one, conv_flat, norm, row_block=256):
    pixels, hidden = d_up.shape
    width = w_one.shape[0]
    return pl.pallas_call(
        norm_back_body,
        grid=(pixels // row_block,),
        in_specs=[
            pl.BlockSpec((row_block, hidden), lambda i: (i, 0)),
            pl.BlockSpec((width, hidden), lambda i: (0, 0)),
            pl.BlockSpec((row_block, width), lambda i: (i, 0)),
            pl.BlockSpec((2, width), lambda i: (0, 0)),
        ],
        out_specs=[
            pl.BlockSpec((row_block, width), lambda i: (i, 0)),
            pl.BlockSpec((2, width), lambda i: (0, 0)),
        ],
        out_shape=[
            jax.ShapeDtypeStruct((pixels, width), F32),
            jax.ShapeDtypeStruct((2, width), F32),
        ],

        cost_estimate=COST,
        name="norm_back",
    )(d_up, w_one, conv_flat, norm)


def branch_out_body(act_ref, w_ref, b_ref, hidden_ref, wet_ref, w_out_ref, b_out_ref, dres_ref, result_ref, gout_ref):
    branch = b_ref[...] + lax.dot_general(
        act_ref[...], w_ref[...], (((1,), (1,)), ((), ())), preferred_element_type=F32
    )
    mixed = ((hidden_ref[...] + branch) * wet_ref[...]).astype(BF16)
    result = jnp.dot(mixed, w_out_ref[...], preferred_element_type=F32) + b_out_ref[...]
    result = result.T
    groups, count, padded_ch, lanes = result_ref.shape
    for row in range(count):
        for g in range(groups):
            piece = result[g * padded_ch : (g + 1) * padded_ch, row * lanes : (row + 1) * lanes]
            result_ref[g, row] = piece.astype(BF16)

    @pl.when(pl.program_id(0) == 0)
    def _():
        gout_ref[...] = jnp.zeros(gout_ref.shape, F32)

    gout_ref[...] += lax.dot_general(
        dres_ref[...], mixed, (((0,), (0,)), ((), ())), preferred_element_type=F32
    )


def branch_out(activated, w_two, b_two, hidden, wet, w_out_slots, b_slots, d_result, out_shape, row_block=256):
    pixels, inner = activated.shape
    width, slots = w_out_slots.shape
    return pl.pallas_call(
        branch_out_body,
        grid=(pixels // row_block,),
        in_specs=[
            pl.BlockSpec((row_block, inner), lambda i: (i, 0)),
            pl.BlockSpec((width, inner), lambda i: (0, 0)),
            pl.BlockSpec((1, width), lambda i: (0, 0)),
            pl.BlockSpec((row_block, width), lambda i: (i, 0)),
            pl.BlockSpec((row_block, 1), lambda i: (i, 0)),
            pl.BlockSpec((width, slots), lambda i: (0, 0)),
            pl.BlockSpec((1, slots), lambda i: (0, 0)),
            pl.BlockSpec((row_block, slots), lambda i: (i, 0)),
        ],
        out_specs=[
            pl.BlockSpec(
                (out_shape[0], row_block // out_shape[3]) + out_shape[2:], lambda i: (0, i, 0, 0)
            ),
            pl.BlockSpec((slots, width), lambda i: (0, 0)),
        ],
        out_shape=[
            jax.ShapeDtypeStruct(out_shape, BF16),
            jax.ShapeDtypeStruct((slots, width), F32),
        ],

        cost_estimate=COST,
        name="branch_out",
    )(activated, w_two, b_two.reshape(1, -1), hidden, wet, w_out_slots, b_slots.reshape(1, -1), d_result)


def conv_back_body(rows, cols, half, edge_ref, coef_ref, dn_ref, conv_ref, dsum_ref, low_ref, depth_ref, dh_ref, dh_low_ref, dh_high_ref, gw_ref, gb_ref, dc_ref, dl_ref, pad_ref, tap_ref):
    kernel = 2 * half + 1
    wide = cols + 2 * half
    d_conv = coef_ref[0:1] * dn_ref[...] + (coef_ref[1:2] * conv_ref[...] + coef_ref[2:3])
    dc_ref[...] = d_conv.astype(BF16).astype(F32)
    dl_ref[...] = jnp.zeros(dl_ref.shape, F32)
    dl_ref[half : half + rows, half : half + cols] = dsum_ref[...]
    pad_ref[...] = low_ref[...].astype(F32).reshape(pad_ref.shape)
    tap_ref[...] = jnp.zeros(tap_ref.shape, F32)

    def one_row(row, carry):
        source = [dc_ref[row, c] for c in range(cols)]
        for i in range(kernel):
            taps = [jnp.broadcast_to(depth_ref[i * kernel + j], (SUBLANES, LANES)) for j in range(kernel)]
            for c in range(wide):
                acc = dl_ref[row + i, c]
                for j in range(kernel):
                    if 0 <= c - j < cols:
                        acc = acc + source[c - j] * taps[j]
                dl_ref[row + i, c] = acc
        for i in range(kernel):
            sums = [tap_ref[i * kernel + j] for j in range(kernel)]
            for c in range(wide):
                value = pad_ref[row + i, c]
                for j in range(kernel):
                    if 0 <= c - j < cols:
                        sums[j] = sums[j] + source[c - j] * value
            for j in range(kernel):
                tap_ref[i * kernel + j] = sums[j]
        return carry

    lax.fori_loop(0, rows, one_row, 0)

    @pl.when(edge_ref[0] == 1)
    def _():
        dl_ref[:half] = jnp.zeros((half,) + dl_ref.shape[1:], F32)

    @pl.when(edge_ref[1] == 1)
    def _():
        dl_ref[half + rows :] = jnp.zeros((half,) + dl_ref.shape[1:], F32)

    @pl.when(edge_ref[2] == 1)
    def _():
        dl_ref[:, :half] = jnp.zeros((dl_ref.shape[0], half) + dl_ref.shape[2:], F32)

    @pl.when(edge_ref[3] == 1)
    def _():
        dl_ref[:, half + cols :] = jnp.zeros((dl_ref.shape[0], half) + dl_ref.shape[2:], F32)

    d_hidden = dl_ref[...]
    dh_ref[...] = d_hidden[:, half : half + cols].reshape(dh_ref.shape).astype(BF16)
    dh_low_ref[...] = d_hidden[:, :half].reshape(dh_low_ref.shape).astype(BF16)
    dh_high_ref[...] = d_hidden[:, half + cols :].reshape(dh_high_ref.shape).astype(BF16)
    gb_ref[...] = jnp.sum(jnp.sum(d_hidden, axis=(0, 1)), axis=0, keepdims=True)
    gw_ref[...] = jnp.sum(tap_ref[...], axis=1)


def conv_back(edges, coef, d_normed, conv_out, d_sum, lowered, depth, tile, first, last, prior=()):
    rows, cols, dates, half = tile
    taps = depth.shape[0]
    width = lowered.shape[1]
    padded = lowered.shape[0]
    inner = pl.BlockSpec((rows, cols, dates, LANES), lambda i: (0, 0, 0, first + i))
    wide = (rows + 2 * half, cols + 2 * half, dates, LANES)
    inside = (rows + 2 * half) * cols * dates
    beside = (rows + 2 * half) * half * dates

    def body(edge_ref, coef_ref, dn_ref, conv_ref, dsum_ref, low_ref, depth_ref, *refs):
        conv_back_body(rows, cols, half, edge_ref, coef_ref, dn_ref, conv_ref, dsum_ref, low_ref, depth_ref, *refs[len(prior) :])

    return pl.pallas_call(
        body,
        grid=(last - first,),
        in_specs=[
            pl.BlockSpec(memory_space=pltpu.SMEM),
            pl.BlockSpec((3, LANES), lambda i: (0, first + i)),
            inner,
            inner,
            inner,
            pl.BlockSpec((padded, LANES), lambda i: (0, first + i)),
            pl.BlockSpec((taps, 1, LANES), lambda i: (0, 0, first + i)),
        ]
        + [pl.BlockSpec(memory_space=pl.ANY)] * len(prior),
        out_specs=[
            pl.BlockSpec((count, LANES), lambda i: (0, first + i)) for count in (inside, beside, beside, taps, 1)
        ],
        out_shape=[
            jax.ShapeDtypeStruct((inside, width), BF16),
            jax.ShapeDtypeStruct((beside, width), BF16),
            jax.ShapeDtypeStruct((beside, width), BF16),
            jax.ShapeDtypeStruct((taps, width), F32),
            jax.ShapeDtypeStruct((1, width), F32),
        ],
        scratch_shapes=[
            pltpu.VMEM((rows, cols, dates, LANES), F32),
            pltpu.VMEM(wide, F32),
            pltpu.VMEM(wide, F32),
            pltpu.VMEM((taps, dates, LANES), F32),
        ],
        input_output_aliases={7 + k: k for k in range(len(prior))},

        cost_estimate=COST,
        name="conv_back",
    )(edges, coef, d_normed, conv_out, d_sum, lowered, depth, *prior)


def input_back(dh, dh_low, dh_high, x, x_low, x_high, w_slots):
    slots, width = w_slots.shape
    inside, beside = dh.shape[0], dh_low.shape[0]
    row_block = inside // 2
    mix = (((1,), (1,)), ((), ()))
    down = (((0,), (0,)), ((), ()))

    def body(dh_ref, dl_ref, dr_ref, x_ref, xl_ref, xr_ref, w_ref, ds_ref, sl_ref, sr_ref, g_ref):
        ds_ref[...] = lax.dot_general(dh_ref[...], w_ref[...], mix, preferred_element_type=F32)

        @pl.when(pl.program_id(0) == 0)
        def _():
            sl_ref[...] = lax.dot_general(
                dl_ref[...], w_ref[...], mix, preferred_element_type=F32
            ).astype(BF16)
            sr_ref[...] = lax.dot_general(
                dr_ref[...], w_ref[...], mix, preferred_element_type=F32
            ).astype(BF16)
            g_ref[...] = lax.dot_general(
                xl_ref[...], dl_ref[...], down, preferred_element_type=F32
            ) + lax.dot_general(xr_ref[...], dr_ref[...], down, preferred_element_type=F32)

        g_ref[...] += lax.dot_general(x_ref[...], dh_ref[...], down, preferred_element_type=F32)

    moving = lambda i: (i, 0)
    fixed = lambda i: (0, 0)
    return pl.pallas_call(
        body,
        grid=(inside // row_block,),
        in_specs=[
            pl.BlockSpec((row_block, width), moving),
            pl.BlockSpec((beside, width), fixed),
            pl.BlockSpec((beside, width), fixed),
            pl.BlockSpec((row_block, slots), moving),
            pl.BlockSpec((beside, slots), fixed),
            pl.BlockSpec((beside, slots), fixed),
            pl.BlockSpec((slots, width), fixed),
        ],
        out_specs=[
            pl.BlockSpec((row_block, slots), moving),
            pl.BlockSpec((beside, slots), fixed),
            pl.BlockSpec((beside, slots), fixed),
            pl.BlockSpec((slots, width), fixed),
        ],
        out_shape=[
            jax.ShapeDtypeStruct((inside, slots), F32),
            jax.ShapeDtypeStruct((beside, slots), BF16),
            jax.ShapeDtypeStruct((beside, slots), BF16),
            jax.ShapeDtypeStruct((slots, width), F32),
        ],
        cost_estimate=COST,
        name="input_back",
    )(dh, dh_low, dh_high, x, x_low, x_high, w_slots)


def to_groups(d_state, from_high, from_low, groups):
    rows, pixels, slots = d_state.shape
    beside = from_low.shape[1]
    padded_ch = slots // groups

    def body(in_ref, high_ref, low_ref, out_ref):
        for row in range(rows):
            value = in_ref[row]
            first = value[:beside] + low_ref[row].astype(F32)
            last = value[pixels - beside :] + high_ref[row].astype(F32)
            value = jnp.concatenate([first, value[beside : pixels - beside], last], axis=0).T
            for g in range(groups):
                out_ref[g, row] = value[g * padded_ch : (g + 1) * padded_ch].astype(BF16)

    return pl.pallas_call(
        body,
        out_shape=jax.ShapeDtypeStruct((groups, rows, padded_ch, pixels), BF16),
        cost_estimate=COST,
        name="to_groups",
    )(d_state, from_high, from_low)


def on_device(
    ocean_state,
    slot_level,
    wet_mask,
    w_in,
    b_in,
    w_depth,
    norm_gain,
    norm_bias,
    w_one,
    b_one,
    w_two,
    b_two,
    w_out,
    b_out,
    cotangent,
):
    groups = lax.axis_size("lev")
    strips = lax.axis_size("sp")
    group_index = lax.axis_index("lev")
    strip_index = lax.axis_index("sp")
    rows, cols = wet_mask.shape
    all_rows, dates, _, group_ch = ocean_state.shape
    padded_ch = -(-group_ch // SUBLANES) * SUBLANES
    slots = padded_ch * groups
    channels, width = w_in.shape
    kernel = w_depth.shape[0]
    half = kernel // 2
    tile = (rows, cols, dates, half)
    high_rows = rows + 2 * half
    pixels = rows * cols * dates
    pixel_total = float(pixels * groups * strips)

    lev_stages = bits_of("lev")
    sp_stages = bits_of("sp")
    stages = lev_stages + sp_stages
    core, lev_rest = lev_stages[:1], lev_stages[1:]
    orders = (
        core + lev_rest + sp_stages,
        core + sp_stages[:1] + lev_rest + sp_stages[1:],
        core + sp_stages[1:2] + lev_rest + sp_stages[:1] + sp_stages[2:],
        core + sp_stages + lev_rest,
    )
    forward = [(i, i + 1) for i in range(strips - 1)]
    backward = [(i + 1, i) for i in range(strips - 1)]
    edges = jnp.stack(
        [group_index == 0, group_index == groups - 1, strip_index == 0, strip_index == strips - 1]
    ).astype(jnp.int32)

    table = slot_table(slot_level, groups, group_ch, padded_ch, channels)
    table_low = table.astype(BF16)
    w_slots = jnp.dot(table_low, w_in, preferred_element_type=F32).astype(BF16)
    w_out_slots = jnp.dot(w_out, table_low.T, preferred_element_type=F32).astype(BF16)
    b_slots = jnp.dot(table, b_out, precision=exact_mode)
    depth = w_depth.astype(F32).reshape(kernel * kernel, 1, width)

    row_pixels = cols * dates
    beside = half * dates
    windows, d_result = to_channel_rows(ocean_state, cotangent, groups, half, padded_ch)
    windows = lax.all_to_all(windows, "lev", split_axis=0, concat_axis=0, tiled=True)
    d_result = lax.all_to_all(
        after(d_result, windows), "lev", split_axis=0, concat_axis=0, tiled=True
    )
    x_rows = to_pixel_rows(windows)
    x_low = lax.ppermute(x_rows[:, row_pixels - beside :], "sp", forward).reshape(-1, slots)
    x_high = lax.ppermute(x_rows[:, :beside], "sp", backward).reshape(-1, slots)
    x_rows = x_rows.reshape(-1, slots)
    d_result = to_pixel_rows(d_result).reshape(pixels, slots)

    hidden, lowered, conv_out, local = hidden_conv(
        edges, x_rows, x_low, x_high, w_slots, b_in, depth, tile
    )
    came = hop(local, stages[0])
    wet = jnp.broadcast_to(
        wet_mask.astype(F32)[:, :, None, None], (rows, cols, dates, 1)
    ).reshape(pixels, 1)
    d_mixed = jnp.dot(d_result, w_out_slots.T, preferred_element_type=F32)
    d_sum = d_mixed * wet
    d_branch = d_sum.astype(BF16)
    g_b_two = jnp.sum(d_branch.astype(F32), axis=0)
    g_bias_slots = jnp.sum(d_result.astype(F32), axis=0)

    sums = butterfly(local + after(came, d_branch), stages[1:])
    mean_value = sums[0] / pixel_total
    inv_scale = lax.rsqrt(sums[1] / pixel_total - mean_value * mean_value + 1e-05)
    conv_flat = conv_out.reshape(pixels, width)
    centered = (conv_flat - mean_value) * inv_scale
    normed = (centered * norm_gain + norm_bias).astype(BF16)
    ff = w_one.shape[1]
    block = 256
    cut = ff // 2 // block * block
    spans = {"a": (cut, ff), "b": (0, cut)}
    flight = Exchanges()

    def as_rows(vector):
        flat = vector.reshape(-1)
        count = -(-flat.shape[0] // width)
        return jnp.pad(flat, (0, count * width - flat.shape[0])).reshape(count, width)

    w_two_t = w_two.T
    core_side = side(core[0])

    def part(name, order, prior=()):
        found, grads = mlp(
            core_side, normed, d_branch, w_one, b_one, w_two_t, *spans[name], prior
        )
        return found, flight.begin(name, grads[0], order, BF16, partner=grads[1])

    found, sent = part("a", orders[0])
    found, sent = part("b", orders[1], (after(found[0], sent),) + found[1:])
    activated, d_up, g_b_one = found
    sent = [sent] + flight.step(g_b_one, "a")

    norm = jnp.stack([mean_value, inv_scale])
    d_normed, parts = norm_back(after(d_up, *sent), w_one, conv_flat, norm)
    sent = flight.step(parts, "b")
    parts = jnp.concatenate(
        [parts, as_rows(g_b_one), as_rows(g_b_two), as_rows(g_bias_slots)], axis=0
    )
    first_hop = hop(parts, stages[0])
    result, g_out_slots = branch_out(
        after(activated, *sent),
        w_two_t,
        b_two,
        hidden.reshape(pixels, width),
        wet,
        w_out_slots,
        b_slots,
        d_result,
        (groups, rows, padded_ch, row_pixels),
    )
    sent = flight.step(g_out_slots, "a")
    result = after(result, *sent)
    next_state = lax.all_to_all(result, "lev", split_axis=0, concat_axis=0, tiled=True)
    first_hop = after(first_hop, g_out_slots, *sent)
    summed = butterfly(parts + first_hop, stages[1:])
    norm_grads = summed[:2]
    sent = flight.step(summed, "b")

    scale = norm_gain * inv_scale
    slope = scale * inv_scale * (norm_grads[1] / pixel_total)
    coef = jnp.stack(
        [scale, -slope, slope * mean_value - scale * (norm_grads[0] / pixel_total)]
    )
    shape4 = (rows, cols, dates, width)
    inputs = (d_normed.reshape(shape4), conv_out, d_sum.reshape(shape4), lowered, depth, tile)
    tiles = pl.cdiv(width, LANES)
    steps = [0, 2, 4, tiles]
    found = ()
    for number, (first, last) in enumerate(zip(steps[:-1], steps[1:])):
        found = conv_back(edges, after(coef, *sent), *inputs, first, last, found)
        if number < 2:
            sent = flight.step(found[4], "b", "a")
    d_hidden, d_low, d_high, g_w_depth, g_b_in = found

    d_state, d_low, d_high, g_in_slots = input_back(
        d_hidden, d_low, d_high, x_rows, x_low, x_high, w_slots
    )
    from_high = lax.ppermute(d_low.reshape(high_rows, beside, slots), "sp", backward)
    from_low = lax.ppermute(d_high.reshape(high_rows, beside, slots), "sp", forward)

    def pack(arrays):
        packed = jnp.concatenate(arrays, axis=0)
        return jnp.pad(packed, ((0, -packed.shape[0] % (16 * SUBLANES)), (0, 0))).reshape(
            -1, SUBLANES, width
        )

    def unpack(packed, arrays):
        packed = packed.reshape(-1, width)
        found = []
        start = 0
        for array in arrays:
            found.append(packed[start : start + array.shape[0]])
            start += array.shape[0]
        return found

    last_sums = [g_out_slots, g_in_slots, g_w_depth, g_b_in]
    sent = [flight.begin("small", pack(last_sums), orders[3], BF16, most=3)]
    sent += flight.step(g_in_slots, "b", "a")
    d_state = to_groups(
        after(d_state, *sent).reshape(high_rows, row_pixels, slots), from_high, from_low, groups
    )
    received = lax.all_to_all(d_state, "lev", split_axis=0, concat_axis=0, tiled=True)
    sent = flight.step(d_state, "small", "b")
    next_state = from_channel_rows(after(next_state, *sent), 0, dates, cols, group_ch)
    sent = flight.step(next_state, "small")
    sent = flight.step(sent[0], "b", "a")
    token = after(sent[0], sent[1])
    sent += flight.step(token, "small")
    grad_ocean_state = from_channel_rows(after(received, *sent), half, dates, cols, group_ch)
    sent = flight.step(grad_ocean_state, "small")
    sent = flight.step(sent[0], "b", "a")
    token = after(sent[0], sent[1])
    sent = flight.step(token, "small")
    flight.finish(sent[0], "b", "a")
    weights = unpack_grads(core_side, flight.done["a"], width, ff, spans["a"][0])
    sent = flight.step(weights[0], "small")
    weights = (after(weights[0], *sent), weights[1])
    weights = unpack_grads(core_side, flight.done["b"], width, ff, spans["b"][0], weights)
    flight.finish(weights[0], "small")
    g_out_slots, g_in_slots, g_w_depth, g_b_in = unpack(in_order(*flight.done["small"]), last_sums)
    grad_w_one, grad_w_two = weights
    grad_w_out = jnp.einsum("sd,sc->dc", g_out_slots.astype(F32), table, precision=exact_mode)
    count = -(-ff // width)
    grad_b_one = summed[2 : 2 + count].reshape(-1)[:ff]
    grad_b_two = summed[2 + count]
    grad_b_out = jnp.dot(summed[3 + count, :slots], table, precision=exact_mode)
    grad_w_in = jnp.dot(table.T, g_in_slots.astype(F32), precision=exact_mode)
    grad_w_depth = g_w_depth.astype(F32).reshape(kernel, kernel, width)
    grad_b_in = g_b_in.astype(F32).reshape(-1)
    return (
        next_state,
        grad_ocean_state,
        grad_w_in,
        grad_b_in,
        grad_w_depth,
        norm_grads[1],
        norm_grads[0],
        grad_w_one,
        grad_b_one,
        grad_w_two.T,
        grad_b_two,
        grad_w_out,
        grad_b_out,
    )


def solution(mesh):
    return jax.shard_map(
        on_device,
        mesh=mesh,
        in_specs=(
            P(None, None, "sp", "lev"),
            P(),
            P("lev", "sp"),
            P(),
            P(),
            P(),
            P(),
            P(),
            P(),
            P(),
            P(),
            P(),
            P(),
            P(),
            P(None, None, "sp", "lev"),
        ),
        out_specs=(
            P(None, None, "sp", "lev"),
            P(None, None, "sp", "lev"),
            P(),
            P(),
            P(),
            P(),
            P(),
            P(),
            P(),
            P(),
            P(),
            P(),
            P(),
        ),
        check_vma=False,
    )
```

```python
import functools

import jax
import jax.numpy as jnp
from jax import lax
from jax.experimental import pallas as pl
from jax.experimental.pallas import tpu as pltpu
from jax.sharding import PartitionSpec as P

VARS = 10
LANES = 128
SUBLANES = 8

exact_mode = lax.Precision.HIGHEST
F32 = jnp.float32
BF16 = jnp.bfloat16

COST = pl.CostEstimate(flops=50000000000, transcendentals=0, bytes_accessed=50000000)

TAIL_SCALE = 0.3
TAIL_POLY = (
    0.119623263,
    0.120845528,
    0.0993471402,
    0.130416391,
    -0.0571672287,
    0.210118226,
    -0.159378204,
    0.0361948279,
)


def slot_table(levels_of_slots, groups, group_ch, padded_ch, channels):
    slot_count = groups * group_ch
    kinds = jnp.arange(slot_count) % VARS
    target = jnp.repeat(levels_of_slots, VARS) * VARS + kinds
    target = jnp.pad(
        target.reshape(groups, group_ch), ((0, 0), (0, padded_ch - group_ch)), constant_values=-1
    ).reshape(-1)
    columns = jnp.arange(channels)
    return (target[:, None] == columns[None, :]).astype(F32)


def bits_of(axis):
    size = lax.axis_size(axis)
    return [(axis, 1 << k) for k in range(size.bit_length() - 1)]


def hop(value, stage):
    axis, bit = stage
    return lax.ppermute(value, axis, [(i, i ^ bit) for i in range(lax.axis_size(axis))])


def side(stage):
    axis, bit = stage
    return (lax.axis_index(axis) // bit) % 2


def butterfly(value, stages):
    for stage in stages:
        value = value + hop(value, stage)
    return value


def after(value, *earlier):
    return lax.optimization_barrier((value,) + earlier)[0]


def halves(value, axis, bit):
    half = value.shape[axis] // 2
    stay = lax.dynamic_slice_in_dim(value, bit * half, half, axis)
    sent = lax.dynamic_slice_in_dim(value, (1 - bit) * half, half, axis)
    return stay, sent


def halving_lanes(lanes):
    tiles = lanes // LANES
    return lanes % LANES == 0 and (tiles % 2 == 0 or tiles >= 9)


def total(terms):
    value = terms[0].astype(F32)
    for term in terms[1:]:
        value = value + term.astype(F32)
    return value


def exchange(value, stages, link, partner=None, most=2):
    kept = []
    own = 0
    lanes = value.shape[2]
    terms = [value]
    rest = stages
    if partner is not None:
        terms.append((yield partner, hop(partner, stages[0])))
        rest = stages[1:]
    row_halvings = 0
    for stage in rest:
        bit = side(stage)
        shape = terms[0].shape
        if stage is rest[-1]:
            axis = None
        elif shape[0] % 2 == 0 and row_halvings < most:
            axis = 0
            row_halvings += 1
            own = own * 2 + bit
        else:
            axis = 2 if halving_lanes(shape[2]) else None
        if axis is None:
            sent = total(terms).astype(link)
            terms = [sent]
        else:
            if axis == 2 and shape[2] // LANES % 2:
                terms = [jnp.pad(term, ((0, 0), (0, 0), (0, LANES))) for term in terms]
            pairs = [halves(term, axis, bit) for term in terms]
            sent = total([pair[1] for pair in pairs]).astype(link)
            terms = [pair[0] for pair in pairs]
            kept.append((stage, axis))
        terms.append((yield sent, hop(sent, stage)))
    value = total(terms).astype(link)
    for stage, axis in reversed(kept):
        came = yield value, hop(value, stage)
        if axis == 0:
            value = jnp.concatenate([value, came], axis=0)
        else:
            bit = side(stage)
            low = jnp.where(bit == 0, value, came)
            high = jnp.where(bit == 0, came, value)
            value = jnp.concatenate([low, high], axis=2)[:, :, :lanes]
    other = None
    if partner is not None:
        other = yield value, hop(value, stages[0])
    yield value, other, own, 1 << row_halvings


def in_order(value, other, own, pieces):
    count = value.shape[0] // pieces
    return jnp.concatenate(
        [lax.dynamic_slice_in_dim(value, (index ^ own) * count, count, 0) for index in range(pieces)],
        axis=0,
    )


class Exchanges:
    def __init__(self):
        self.running = {}
        self.came = {}
        self.done = {}

    def hold(self, name, got):
        if len(got) == 2:
            self.came[name] = got[1]
            return [got[0]]
        self.done[name] = got
        del self.running[name]
        return []

    def begin(self, name, *args, **options):
        self.running[name] = exchange(*args, **options)
        return self.hold(name, next(self.running[name]))[0]

    def step(self, token, *names, joint=False):
        names = [name for name in names if name in self.running]
        if joint:
            came = lax.optimization_barrier(tuple(self.came[name] for name in names) + (token,))
        else:
            came = [after(self.came[name], token) for name in names]
        sent = []
        for name, value in zip(names, came):
            sent += self.hold(name, self.running[name].send(value))
        return sent

    def finish(self, token, *names):
        while any(name in self.running for name in names):
            self.step(token, *names)


def unpack_grads(core_side, reduced, width, ff, start, prior=()):
    value, other, own, pieces = reduced
    count = value.shape[0] // pieces
    rows = count * SUBLANES
    columns = value.shape[2]

    def body(own_ref, value_ref, other_ref, *refs):
        out_one, out_two = refs[len(prior) :]
        mine = value_ref[...].astype(F32).reshape(rows, columns)
        theirs = other_ref[...].astype(F32).reshape(rows, columns)
        first = own_ref[1] == 0

        @pl.when(first)
        def _():
            out_one[...] = mine
            out_two[...] = theirs

        @pl.when(jnp.logical_not(first))
        def _():
            out_one[...] = theirs
            out_two[...] = mine

    out = pl.BlockSpec((pl.Element(rows), pl.Element(columns)), lambda i, own: (i * rows, start))
    piece = pl.BlockSpec((count, SUBLANES, columns), lambda i, own: (i ^ own[0], 0, 0))
    return pl.pallas_call(
        body,
        grid_spec=pltpu.PrefetchScalarGridSpec(
            num_scalar_prefetch=1,
            grid=(pieces,),
            in_specs=[piece, piece] + [pl.BlockSpec(memory_space=pl.ANY)] * len(prior),
            out_specs=[out, out],
        ),
        out_shape=[jax.ShapeDtypeStruct((width, ff), F32)] * 2,
        input_output_aliases={3 + k: k for k in range(len(prior))},
        cost_estimate=COST,
        name="unpack_grads",
    )(jnp.stack([own, core_side]).astype(jnp.int32), value, other, *prior)


def pixel_order(dates, cols):
    pixels = dates * cols
    source = lax.broadcasted_iota(jnp.int32, (pixels, pixels), 0)
    place = lax.broadcasted_iota(jnp.int32, (pixels, pixels), 1)
    return ((source % cols) * dates + source // cols == place).astype(BF16)


def to_channel_rows(state, cotangent, groups, half, padded_ch):
    all_rows, dates, cols, ch = state.shape
    rows = all_rows // groups
    high = rows + 2 * half
    pixels = dates * cols

    def body(state_ref, cot_ref, window_ref, ct_ref):
        perm = pixel_order(dates, cols)
        blank = jnp.zeros((padded_ch - ch, pixels), F32)
        zero = jnp.zeros((padded_ch, pixels), BF16)

        def turned(ref, row):
            value = lax.dot_general(
                ref[row].reshape(pixels, ch), perm, (((0,), (0,)), ((), ())), preferred_element_type=F32
            )
            return jnp.concatenate([value, blank], axis=0).astype(BF16) if padded_ch > ch else value.astype(BF16)

        for row in range(half):
            window_ref[0, row] = zero
            window_ref[groups - 1, half + rows + row] = zero
        for row in range(all_rows):
            value = turned(state_ref, row)
            for band in range(groups):
                place = row - band * rows + half
                if 0 <= place < high:
                    window_ref[band, place] = value
            ct_ref[row // rows, row % rows] = turned(cot_ref, row)

    return pl.pallas_call(
        body,
        out_shape=[
            jax.ShapeDtypeStruct((groups, high, padded_ch, pixels), BF16),
            jax.ShapeDtypeStruct((groups, rows, padded_ch, pixels), BF16),
        ],
        cost_estimate=COST,
        name="to_channel_rows",
    )(state, cotangent)


def from_channel_rows(windows, half, dates, cols, ch):
    groups, high, padded_ch, pixels = windows.shape
    rows = high - 2 * half

    def body(window_ref, out_ref):
        perm = pixel_order(dates, cols)
        for row in range(groups * rows):
            value = None
            for band in range(groups):
                place = row - band * rows + half
                if 0 <= place < high:
                    piece = window_ref[band, place]
                    value = piece if value is None else value.astype(F32) + piece.astype(F32)
            value = lax.dot_general(
                perm, value.astype(BF16), (((1,), (1,)), ((), ())), preferred_element_type=F32
            )
            out_ref[row] = value[:, :ch].astype(BF16).reshape(dates, cols, ch)

    return pl.pallas_call(
        body,
        out_shape=jax.ShapeDtypeStruct((groups * rows, dates, cols, ch), BF16),
        cost_estimate=COST,
        name="from_channel_rows",
    )(windows)


def to_pixel_rows(received):
    groups, rows, padded_ch, pixels = received.shape
    slots = groups * padded_ch

    def body(in_ref, out_ref):
        for row in range(rows):
            value = jnp.concatenate([in_ref[g, row].astype(F32) for g in range(groups)], axis=0)
            out_ref[row] = value.T.astype(BF16)

    return pl.pallas_call(
        body,
        out_shape=jax.ShapeDtypeStruct((rows, pixels, slots), BF16),
        cost_estimate=COST,
        name="to_pixel_rows",
    )(received)


def hidden_conv_body(rows, cols, half, edge_ref, x_ref, low_x_ref, high_x_ref, w_ref, b_ref, depth_ref, hidden_ref, low_ref, conv_ref, stat_ref, pad_ref):
    kernel = 2 * half + 1
    high = rows + 2 * half

    def hidden_of(ref, columns):
        value = jnp.dot(ref[...], w_ref[...], preferred_element_type=F32) + b_ref[...]
        return value.reshape(high, columns, SUBLANES, LANES)

    value = hidden_of(x_ref, cols)
    hidden_ref[...] = value[half : half + rows]
    pad_ref[:, half : half + cols] = value.astype(BF16).astype(F32)
    pad_ref[:, :half] = hidden_of(low_x_ref, half).astype(BF16).astype(F32)
    pad_ref[:, half + cols :] = hidden_of(high_x_ref, half).astype(BF16).astype(F32)

    @pl.when(edge_ref[0] == 1)
    def _():
        pad_ref[:half] = jnp.zeros((half,) + pad_ref.shape[1:], F32)

    @pl.when(edge_ref[1] == 1)
    def _():
        pad_ref[half + rows :] = jnp.zeros((half,) + pad_ref.shape[1:], F32)

    @pl.when(edge_ref[2] == 1)
    def _():
        pad_ref[:, :half] = jnp.zeros((pad_ref.shape[0], half) + pad_ref.shape[2:], F32)

    @pl.when(edge_ref[3] == 1)
    def _():
        pad_ref[:, half + cols :] = jnp.zeros((pad_ref.shape[0], half) + pad_ref.shape[2:], F32)

    low_ref[...] = pad_ref[...].reshape(low_ref.shape).astype(BF16)

    def one_row(row, carry):
        total, square = carry
        acc = jnp.zeros((cols, SUBLANES, LANES), F32)
        for i in range(kernel):
            slab = pad_ref[row + i]
            for j in range(kernel):
                acc = acc + slab[j : j + cols] * depth_ref[i * kernel + j]
        conv_ref[row] = acc
        return total + jnp.sum(acc, axis=0), square + jnp.sum(acc * acc, axis=0)

    zero = jnp.zeros((SUBLANES, LANES), F32)
    total, square = lax.fori_loop(0, rows, one_row, (zero, zero))
    stat_ref[0:1] = jnp.sum(total, axis=0, keepdims=True)
    stat_ref[1:2] = jnp.sum(square, axis=0, keepdims=True)


def hidden_conv(edges, x, low_x, high_x, w_slots, b_in, depth, tile):
    rows, cols, dates, half = tile
    slots, width = w_slots.shape
    padded = (rows + 2 * half) * (cols + 2 * half) * dates
    return pl.pallas_call(
        functools.partial(hidden_conv_body, rows, cols, half),
        grid=(pl.cdiv(width, LANES),),
        in_specs=[
            pl.BlockSpec(memory_space=pltpu.SMEM),
            pl.BlockSpec(x.shape, lambda i: (0, 0)),
            pl.BlockSpec(low_x.shape, lambda i: (0, 0)),
            pl.BlockSpec(high_x.shape, lambda i: (0, 0)),
            pl.BlockSpec((slots, LANES), lambda i: (0, i)),
            pl.BlockSpec((1, LANES), lambda i: (0, i)),
            pl.BlockSpec((depth.shape[0], 1, LANES), lambda i: (0, 0, i)),
        ],
        out_specs=[
            pl.BlockSpec((rows, cols, dates, LANES), lambda i: (0, 0, 0, i)),
            pl.BlockSpec((padded, LANES), lambda i: (0, i)),
            pl.BlockSpec((rows, cols, dates, LANES), lambda i: (0, 0, 0, i)),
            pl.BlockSpec((2, LANES), lambda i: (0, i)),
        ],
        out_shape=[
            jax.ShapeDtypeStruct((rows, cols, dates, width), F32),
            jax.ShapeDtypeStruct((padded, width), BF16),
            jax.ShapeDtypeStruct((rows, cols, dates, width), F32),
            jax.ShapeDtypeStruct((2, width), F32),
        ],
        scratch_shapes=[pltpu.VMEM((rows + 2 * half, cols + 2 * half, dates, LANES), F32)],

        cost_estimate=COST,
        name="hidden_conv",
    )(edges, x, low_x, high_x, w_slots, b_in.reshape(1, -1), depth)


def gelu_pair(values):
    size = jnp.abs(values)
    gauss = jnp.exp(-0.5 * values * values)
    t = 1.0 / (1.0 + TAIL_SCALE * size)
    poly = jnp.full_like(t, TAIL_POLY[-1])
    for factor in TAIL_POLY[-2::-1]:
        poly = poly * t + factor
    tail = gauss * (t * poly)
    below = jnp.where(values >= 0, 1.0 - tail, tail)
    return values * below, below + values * (gauss * 0.3989422804014327)


def mlp_body(row_block, core_ref, normed_ref, branch_ref, w_one_ref, b_one_ref, w_two_ref, act_ref, dup_ref, keep_ref, send_ref, gb_ref, normed_t, branch_t):
    @pl.when(pl.program_id(0) == 0)
    def _():
        normed_t[...] = normed_ref[...].T
        branch_t[...] = branch_ref[...].T

    total = jnp.zeros((1, act_ref.shape[1]), F32)
    for start in range(0, normed_ref.shape[0], row_block):
        rows = pl.ds(start, row_block)
        up = jnp.dot(normed_ref[rows], w_one_ref[...], preferred_element_type=F32) + b_one_ref[...]
        d_act = jnp.dot(branch_ref[rows], w_two_ref[...], preferred_element_type=F32)
        value, slope = gelu_pair(up)
        act_ref[rows] = value.astype(BF16)
        d_up = (slope * d_act).astype(BF16)
        dup_ref[rows] = d_up
        total = total + jnp.sum(d_up.astype(F32), axis=0, keepdims=True)
    gb_ref[...] = total
    grad_one = jnp.dot(normed_t[...], dup_ref[...], preferred_element_type=F32).astype(BF16)
    grad_two = jnp.dot(branch_t[...], act_ref[...], preferred_element_type=F32).astype(BF16)
    first = core_ref[0] == 0

    @pl.when(first)
    def _():
        keep_ref[...] = grad_one
        send_ref[...] = grad_two

    @pl.when(jnp.logical_not(first))
    def _():
        keep_ref[...] = grad_two
        send_ref[...] = grad_one


def mlp(core_side, normed, d_branch, w_one, b_one, w_two, first, last, prior=(), block=256, row_block=128):
    pixels, width = normed.shape
    hidden = w_one.shape[1]
    start = first // block

    def body(core_ref, normed_ref, branch_ref, w_one_ref, b_one_ref, w_two_ref, *refs):
        mlp_body(row_block, core_ref, normed_ref, branch_ref, w_one_ref, b_one_ref, w_two_ref, *refs[len(prior) :])

    whole = jax.ShapeDtypeStruct((pixels, hidden), BF16)
    grad = jax.ShapeDtypeStruct((width, last - first), BF16)
    results = pl.pallas_call(
        body,
        grid=(pl.cdiv(last - first, block),),
        in_specs=[
            pl.BlockSpec(memory_space=pltpu.SMEM),
            pl.BlockSpec((pixels, width), lambda i: (0, 0)),
            pl.BlockSpec((pixels, width), lambda i: (0, 0)),
            pl.BlockSpec((width, block), lambda i: (0, start + i)),
            pl.BlockSpec((1, block), lambda i: (0, start + i)),
            pl.BlockSpec((width, block), lambda i: (0, start + i)),
        ]
        + [pl.BlockSpec(memory_space=pl.ANY)] * len(prior),
        out_specs=[
            pl.BlockSpec((pixels, block), lambda i: (0, start + i)),
            pl.BlockSpec((pixels, block), lambda i: (0, start + i)),
            pl.BlockSpec((width, block), lambda i: (0, i)),
            pl.BlockSpec((width, block), lambda i: (0, i)),
            pl.BlockSpec((1, block), lambda i: (0, start + i)),
        ],
        out_shape=[whole, whole, grad, grad, jax.ShapeDtypeStruct((1, hidden), F32)],
        scratch_shapes=[pltpu.VMEM((width, pixels), BF16), pltpu.VMEM((width, pixels), BF16)],
        input_output_aliases={6 + n: k for n, k in enumerate((0, 1, 4)[: len(prior)])},

        cost_estimate=COST,
        name="mlp",
    )(core_side.reshape(1).astype(jnp.int32), normed, d_branch, w_one, b_one.reshape(1, -1), w_two, *prior)
    activated, d_up, keep, send, bias = results
    blocks = (width // SUBLANES, SUBLANES, last - first)
    return (activated, d_up, bias), (keep.reshape(blocks), send.reshape(blocks))


def norm_back_body(dup_ref, w_ref, conv_ref, norm_ref, dn_ref, part_ref):
    value = lax.dot_general(
        dup_ref[...], w_ref[...], (((1,), (1,)), ((), ())), preferred_element_type=F32
    )
    dn_ref[...] = value
    centered = (conv_ref[...] - norm_ref[0:1]) * norm_ref[1:2]

    @pl.when(pl.program_id(0) == 0)
    def _():
        part_ref[...] = jnp.zeros(part_ref.shape, F32)

    part_ref[0:1] += jnp.sum(value, axis=0, keepdims=True)
    part_ref[1:2] += jnp.sum(value * centered, axis=0, keepdims=True)


def norm_back(d_up, w_one, conv_flat, norm, row_block=256):
    pixels, hidden = d_up.shape
    width = w_one.shape[0]
    return pl.pallas_call(
        norm_back_body,
        grid=(pixels // row_block,),
        in_specs=[
            pl.BlockSpec((row_block, hidden), lambda i: (i, 0)),
            pl.BlockSpec((width, hidden), lambda i: (0, 0)),
            pl.BlockSpec((row_block, width), lambda i: (i, 0)),
            pl.BlockSpec((2, width), lambda i: (0, 0)),
        ],
        out_specs=[
            pl.BlockSpec((row_block, width), lambda i: (i, 0)),
            pl.BlockSpec((2, width), lambda i: (0, 0)),
        ],
        out_shape=[
            jax.ShapeDtypeStruct((pixels, width), F32),
            jax.ShapeDtypeStruct((2, width), F32),
        ],

        cost_estimate=COST,
        name="norm_back",
    )(d_up, w_one, conv_flat, norm)


def branch_out_body(act_ref, w_ref, b_ref, hidden_ref, wet_ref, w_out_ref, b_out_ref, dres_ref, result_ref, gout_ref):
    branch = b_ref[...] + lax.dot_general(
        act_ref[...], w_ref[...], (((1,), (1,)), ((), ())), preferred_element_type=F32
    )
    mixed = ((hidden_ref[...] + branch) * wet_ref[...]).astype(BF16)
    result = jnp.dot(mixed, w_out_ref[...], preferred_element_type=F32) + b_out_ref[...]
    result = result.T
    groups, count, padded_ch, lanes = result_ref.shape
    for row in range(count):
        for g in range(groups):
            piece = result[g * padded_ch : (g + 1) * padded_ch, row * lanes : (row + 1) * lanes]
            result_ref[g, row] = piece.astype(BF16)

    @pl.when(pl.program_id(0) == 0)
    def _():
        gout_ref[...] = jnp.zeros(gout_ref.shape, F32)

    gout_ref[...] += lax.dot_general(
        dres_ref[...], mixed, (((0,), (0,)), ((), ())), preferred_element_type=F32
    )


def branch_out(activated, w_two, b_two, hidden, wet, w_out_slots, b_slots, d_result, out_shape, row_block=256):
    pixels, inner = activated.shape
    width, slots = w_out_slots.shape
    return pl.pallas_call(
        branch_out_body,
        grid=(pixels // row_block,),
        in_specs=[
            pl.BlockSpec((row_block, inner), lambda i: (i, 0)),
            pl.BlockSpec((width, inner), lambda i: (0, 0)),
            pl.BlockSpec((1, width), lambda i: (0, 0)),
            pl.BlockSpec((row_block, width), lambda i: (i, 0)),
            pl.BlockSpec((row_block, 1), lambda i: (i, 0)),
            pl.BlockSpec((width, slots), lambda i: (0, 0)),
            pl.BlockSpec((1, slots), lambda i: (0, 0)),
            pl.BlockSpec((row_block, slots), lambda i: (i, 0)),
        ],
        out_specs=[
            pl.BlockSpec(
                (out_shape[0], row_block // out_shape[3]) + out_shape[2:], lambda i: (0, i, 0, 0)
            ),
            pl.BlockSpec((slots, width), lambda i: (0, 0)),
        ],
        out_shape=[
            jax.ShapeDtypeStruct(out_shape, BF16),
            jax.ShapeDtypeStruct((slots, width), F32),
        ],

        cost_estimate=COST,
        name="branch_out",
    )(activated, w_two, b_two.reshape(1, -1), hidden, wet, w_out_slots, b_slots.reshape(1, -1), d_result)


def conv_back_body(rows, cols, half, edge_ref, coef_ref, dn_ref, conv_ref, dsum_ref, low_ref, depth_ref, dh_ref, dh_low_ref, dh_high_ref, gw_ref, gb_ref, dc_ref, dl_ref, pad_ref, tap_ref):
    kernel = 2 * half + 1
    wide = cols + 2 * half
    d_conv = coef_ref[0:1] * dn_ref[...] + (coef_ref[1:2] * conv_ref[...] + coef_ref[2:3])
    dc_ref[...] = d_conv.astype(BF16).astype(F32)
    dl_ref[...] = jnp.zeros(dl_ref.shape, F32)
    dl_ref[half : half + rows, half : half + cols] = dsum_ref[...]
    pad_ref[...] = low_ref[...].astype(F32).reshape(pad_ref.shape)
    tap_ref[...] = jnp.zeros(tap_ref.shape, F32)

    def one_row(row, carry):
        source = [dc_ref[row, c] for c in range(cols)]
        for i in range(kernel):
            taps = [jnp.broadcast_to(depth_ref[i * kernel + j], (SUBLANES, LANES)) for j in range(kernel)]
            for c in range(wide):
                acc = dl_ref[row + i, c]
                for j in range(kernel):
                    if 0 <= c - j < cols:
                        acc = acc + source[c - j] * taps[j]
                dl_ref[row + i, c] = acc
        for i in range(kernel):
            sums = [tap_ref[i * kernel + j] for j in range(kernel)]
            for c in range(wide):
                value = pad_ref[row + i, c]
                for j in range(kernel):
                    if 0 <= c - j < cols:
                        sums[j] = sums[j] + source[c - j] * value
            for j in range(kernel):
                tap_ref[i * kernel + j] = sums[j]
        return carry

    lax.fori_loop(0, rows, one_row, 0)

    @pl.when(edge_ref[0] == 1)
    def _():
        dl_ref[:half] = jnp.zeros((half,) + dl_ref.shape[1:], F32)

    @pl.when(edge_ref[1] == 1)
    def _():
        dl_ref[half + rows :] = jnp.zeros((half,) + dl_ref.shape[1:], F32)

    @pl.when(edge_ref[2] == 1)
    def _():
        dl_ref[:, :half] = jnp.zeros((dl_ref.shape[0], half) + dl_ref.shape[2:], F32)

    @pl.when(edge_ref[3] == 1)
    def _():
        dl_ref[:, half + cols :] = jnp.zeros((dl_ref.shape[0], half) + dl_ref.shape[2:], F32)

    d_hidden = dl_ref[...]
    dh_ref[...] = d_hidden[:, half : half + cols].reshape(dh_ref.shape).astype(BF16)
    dh_low_ref[...] = d_hidden[:, :half].reshape(dh_low_ref.shape).astype(BF16)
    dh_high_ref[...] = d_hidden[:, half + cols :].reshape(dh_high_ref.shape).astype(BF16)
    gb_ref[...] = jnp.sum(jnp.sum(d_hidden, axis=(0, 1)), axis=0, keepdims=True)
    gw_ref[...] = jnp.sum(tap_ref[...], axis=1)


def conv_back(edges, coef, d_normed, conv_out, d_sum, lowered, depth, tile, first, last, prior=()):
    rows, cols, dates, half = tile
    taps = depth.shape[0]
    width = lowered.shape[1]
    padded = lowered.shape[0]
    inner = pl.BlockSpec((rows, cols, dates, LANES), lambda i: (0, 0, 0, first + i))
    wide = (rows + 2 * half, cols + 2 * half, dates, LANES)
    inside = (rows + 2 * half) * cols * dates
    beside = (rows + 2 * half) * half * dates

    def body(edge_ref, coef_ref, dn_ref, conv_ref, dsum_ref, low_ref, depth_ref, *refs):
        conv_back_body(rows, cols, half, edge_ref, coef_ref, dn_ref, conv_ref, dsum_ref, low_ref, depth_ref, *refs[len(prior) :])

    return pl.pallas_call(
        body,
        grid=(last - first,),
        in_specs=[
            pl.BlockSpec(memory_space=pltpu.SMEM),
            pl.BlockSpec((3, LANES), lambda i: (0, first + i)),
            inner,
            inner,
            inner,
            pl.BlockSpec((padded, LANES), lambda i: (0, first + i)),
            pl.BlockSpec((taps, 1, LANES), lambda i: (0, 0, first + i)),
        ]
        + [pl.BlockSpec(memory_space=pl.ANY)] * len(prior),
        out_specs=[
            pl.BlockSpec((count, LANES), lambda i: (0, first + i)) for count in (inside, beside, beside, taps, 1)
        ],
        out_shape=[
            jax.ShapeDtypeStruct((inside, width), BF16),
            jax.ShapeDtypeStruct((beside, width), BF16),
            jax.ShapeDtypeStruct((beside, width), BF16),
            jax.ShapeDtypeStruct((taps, width), F32),
            jax.ShapeDtypeStruct((1, width), F32),
        ],
        scratch_shapes=[
            pltpu.VMEM((rows, cols, dates, LANES), F32),
            pltpu.VMEM(wide, F32),
            pltpu.VMEM(wide, F32),
            pltpu.VMEM((taps, dates, LANES), F32),
        ],
        input_output_aliases={7 + k: k for k in range(len(prior))},

        cost_estimate=COST,
        name="conv_back",
    )(edges, coef, d_normed, conv_out, d_sum, lowered, depth, *prior)


def input_back(dh, dh_low, dh_high, x, x_low, x_high, w_slots):
    slots, width = w_slots.shape
    inside, beside = dh.shape[0], dh_low.shape[0]
    row_block = inside // 2
    mix = (((1,), (1,)), ((), ()))
    down = (((0,), (0,)), ((), ()))

    def body(dh_ref, dl_ref, dr_ref, x_ref, xl_ref, xr_ref, w_ref, ds_ref, sl_ref, sr_ref, g_ref):
        ds_ref[...] = lax.dot_general(dh_ref[...], w_ref[...], mix, preferred_element_type=F32)

        @pl.when(pl.program_id(0) == 0)
        def _():
            sl_ref[...] = lax.dot_general(
                dl_ref[...], w_ref[...], mix, preferred_element_type=F32
            ).astype(BF16)
            sr_ref[...] = lax.dot_general(
                dr_ref[...], w_ref[...], mix, preferred_element_type=F32
            ).astype(BF16)
            g_ref[...] = lax.dot_general(
                xl_ref[...], dl_ref[...], down, preferred_element_type=F32
            ) + lax.dot_general(xr_ref[...], dr_ref[...], down, preferred_element_type=F32)

        g_ref[...] += lax.dot_general(x_ref[...], dh_ref[...], down, preferred_element_type=F32)

    moving = lambda i: (i, 0)
    fixed = lambda i: (0, 0)
    return pl.pallas_call(
        body,
        grid=(inside // row_block,),
        in_specs=[
            pl.BlockSpec((row_block, width), moving),
            pl.BlockSpec((beside, width), fixed),
            pl.BlockSpec((beside, width), fixed),
            pl.BlockSpec((row_block, slots), moving),
            pl.BlockSpec((beside, slots), fixed),
            pl.BlockSpec((beside, slots), fixed),
            pl.BlockSpec((slots, width), fixed),
        ],
        out_specs=[
            pl.BlockSpec((row_block, slots), moving),
            pl.BlockSpec((beside, slots), fixed),
            pl.BlockSpec((beside, slots), fixed),
            pl.BlockSpec((slots, width), fixed),
        ],
        out_shape=[
            jax.ShapeDtypeStruct((inside, slots), F32),
            jax.ShapeDtypeStruct((beside, slots), BF16),
            jax.ShapeDtypeStruct((beside, slots), BF16),
            jax.ShapeDtypeStruct((slots, width), F32),
        ],
        cost_estimate=COST,
        name="input_back",
    )(dh, dh_low, dh_high, x, x_low, x_high, w_slots)


def to_groups(d_state, from_high, from_low, groups):
    rows, pixels, slots = d_state.shape
    beside = from_low.shape[1]
    padded_ch = slots // groups

    def body(in_ref, high_ref, low_ref, out_ref):
        for row in range(rows):
            value = in_ref[row]
            first = value[:beside] + low_ref[row].astype(F32)
            last = value[pixels - beside :] + high_ref[row].astype(F32)
            value = jnp.concatenate([first, value[beside : pixels - beside], last], axis=0).T
            for g in range(groups):
                out_ref[g, row] = value[g * padded_ch : (g + 1) * padded_ch].astype(BF16)

    return pl.pallas_call(
        body,
        out_shape=jax.ShapeDtypeStruct((groups, rows, padded_ch, pixels), BF16),
        cost_estimate=COST,
        name="to_groups",
    )(d_state, from_high, from_low)


def on_device(
    ocean_state,
    slot_level,
    wet_mask,
    w_in,
    b_in,
    w_depth,
    norm_gain,
    norm_bias,
    w_one,
    b_one,
    w_two,
    b_two,
    w_out,
    b_out,
    cotangent,
):
    groups = lax.axis_size("lev")
    strips = lax.axis_size("sp")
    group_index = lax.axis_index("lev")
    strip_index = lax.axis_index("sp")
    rows, cols = wet_mask.shape
    all_rows, dates, _, group_ch = ocean_state.shape
    padded_ch = -(-group_ch // SUBLANES) * SUBLANES
    slots = padded_ch * groups
    channels, width = w_in.shape
    kernel = w_depth.shape[0]
    half = kernel // 2
    tile = (rows, cols, dates, half)
    high_rows = rows + 2 * half
    pixels = rows * cols * dates
    pixel_total = float(pixels * groups * strips)

    lev_stages = bits_of("lev")
    sp_stages = bits_of("sp")
    stages = lev_stages + sp_stages
    core, lev_rest = lev_stages[:1], lev_stages[1:]
    orders = (
        core + lev_rest + sp_stages,
        core + sp_stages[:1] + lev_rest + sp_stages[1:],
        core + sp_stages[1:2] + lev_rest + sp_stages[:1] + sp_stages[2:],
        core + sp_stages[1:] + sp_stages[:1] + lev_rest,
    )
    forward = [(i, i + 1) for i in range(strips - 1)]
    backward = [(i + 1, i) for i in range(strips - 1)]
    edges = jnp.stack(
        [group_index == 0, group_index == groups - 1, strip_index == 0, strip_index == strips - 1]
    ).astype(jnp.int32)

    table = slot_table(slot_level, groups, group_ch, padded_ch, channels)
    table_low = table.astype(BF16)
    w_slots = jnp.dot(table_low, w_in, preferred_element_type=F32).astype(BF16)
    w_out_slots = jnp.dot(w_out, table_low.T, preferred_element_type=F32).astype(BF16)
    b_slots = jnp.dot(table, b_out, precision=exact_mode)
    depth = w_depth.astype(F32).reshape(kernel * kernel, 1, width)

    row_pixels = cols * dates
    beside = half * dates
    windows, d_result = to_channel_rows(ocean_state, cotangent, groups, half, padded_ch)
    windows = lax.all_to_all(windows, "lev", split_axis=0, concat_axis=0, tiled=True)
    d_result = lax.all_to_all(
        after(d_result, windows), "lev", split_axis=0, concat_axis=0, tiled=True
    )
    x_rows = to_pixel_rows(windows)
    x_low = lax.ppermute(x_rows[:, row_pixels - beside :], "sp", forward).reshape(-1, slots)
    x_high = lax.ppermute(x_rows[:, :beside], "sp", backward).reshape(-1, slots)
    x_rows = x_rows.reshape(-1, slots)
    d_result = to_pixel_rows(d_result).reshape(pixels, slots)

    hidden, lowered, conv_out, local = hidden_conv(
        edges, x_rows, x_low, x_high, w_slots, b_in, depth, tile
    )
    came = hop(local, stages[0])
    wet = jnp.broadcast_to(
        wet_mask.astype(F32)[:, :, None, None], (rows, cols, dates, 1)
    ).reshape(pixels, 1)
    d_mixed = jnp.dot(d_result, w_out_slots.T, preferred_element_type=F32)
    d_sum = d_mixed * wet
    d_branch = d_sum.astype(BF16)
    g_b_two = jnp.sum(d_branch.astype(F32), axis=0)
    g_bias_slots = jnp.sum(d_result.astype(F32), axis=0)

    sums = butterfly(local + after(came, d_branch), stages[1:])
    mean_value = sums[0] / pixel_total
    inv_scale = lax.rsqrt(sums[1] / pixel_total - mean_value * mean_value + 1e-05)
    conv_flat = conv_out.reshape(pixels, width)
    centered = (conv_flat - mean_value) * inv_scale
    normed = (centered * norm_gain + norm_bias).astype(BF16)
    ff = w_one.shape[1]
    block = 256
    cut = ff // 2 // block * block
    spans = {"a": (cut, ff), "b": (0, cut)}
    flight = Exchanges()

    def as_rows(vector):
        flat = vector.reshape(-1)
        count = -(-flat.shape[0] // width)
        return jnp.pad(flat, (0, count * width - flat.shape[0])).reshape(count, width)

    w_two_t = w_two.T
    core_side = side(core[0])

    def part(name, order, prior=()):
        found, grads = mlp(
            core_side, normed, d_branch, w_one, b_one, w_two_t, *spans[name], prior
        )
        return found, flight.begin(name, grads[0], order, BF16, partner=grads[1])

    found, sent = part("a", orders[0])
    found, sent = part("b", orders[1], (after(found[0], sent),) + found[1:])
    activated, d_up, g_b_one = found
    sent = [sent] + flight.step(g_b_one, "a")

    norm = jnp.stack([mean_value, inv_scale])
    d_normed, parts = norm_back(after(d_up, *sent), w_one, conv_flat, norm)
    sent = flight.step(parts, "b")
    parts = jnp.concatenate(
        [parts, as_rows(g_b_one), as_rows(g_b_two), as_rows(g_bias_slots)], axis=0
    )
    first_hop = hop(parts, stages[0])
    result, g_out_slots = branch_out(
        after(activated, *sent),
        w_two_t,
        b_two,
        hidden.reshape(pixels, width),
        wet,
        w_out_slots,
        b_slots,
        d_result,
        (groups, rows, padded_ch, row_pixels),
    )
    sent = flight.step(g_out_slots, "a")
    result = after(result, *sent)
    next_state = lax.all_to_all(result, "lev", split_axis=0, concat_axis=0, tiled=True)
    first_hop = after(first_hop, g_out_slots, *sent)
    summed = butterfly(parts + first_hop, stages[1:])
    norm_grads = summed[:2]
    sent = flight.step(summed, "b")

    scale = norm_gain * inv_scale
    slope = scale * inv_scale * (norm_grads[1] / pixel_total)
    coef = jnp.stack(
        [scale, -slope, slope * mean_value - scale * (norm_grads[0] / pixel_total)]
    )
    shape4 = (rows, cols, dates, width)
    inputs = (d_normed.reshape(shape4), conv_out, d_sum.reshape(shape4), lowered, depth, tile)
    tiles = pl.cdiv(width, LANES)
    steps = [0, tiles - 4, tiles - 2, tiles]
    found = ()
    for number, (first, last) in enumerate(zip(steps[:-1], steps[1:])):
        found = conv_back(edges, after(coef, *sent), *inputs, first, last, found)
        if number < 2:
            sent = flight.step(found[4], "b", "a")
    d_hidden, d_low, d_high, g_w_depth, g_b_in = found

    d_state, d_low, d_high, g_in_slots = input_back(
        d_hidden, d_low, d_high, x_rows, x_low, x_high, w_slots
    )
    from_high = lax.ppermute(d_low.reshape(high_rows, beside, slots), "sp", backward)
    from_low = lax.ppermute(d_high.reshape(high_rows, beside, slots), "sp", forward)

    def pack(arrays):
        packed = jnp.concatenate(arrays, axis=0)
        return jnp.pad(packed, ((0, -packed.shape[0] % (16 * SUBLANES)), (0, 0))).reshape(
            -1, SUBLANES, width
        )

    def unpack(packed, arrays):
        packed = packed.reshape(-1, width)
        found = []
        start = 0
        for array in arrays:
            found.append(packed[start : start + array.shape[0]])
            start += array.shape[0]
        return found

    last_sums = [g_out_slots, g_in_slots, g_w_depth, g_b_in]
    sent = [flight.begin("small", pack(last_sums), orders[3], BF16, most=3)]
    sent += flight.step(g_in_slots, "b", "a")
    d_state = to_groups(
        after(d_state, *sent).reshape(high_rows, row_pixels, slots), from_high, from_low, groups
    )
    sent = flight.step(d_state, "small")
    sent = flight.step(sent[0], "b", "a", joint=True)
    next_state = from_channel_rows(after(next_state, *sent), 0, dates, cols, group_ch)
    sent = flight.step(next_state, "small")
    sent = flight.step(sent[0], "b", "a", joint=True)
    token = after(sent[0], sent[1])
    received = lax.all_to_all(
        after(d_state, token), "lev", split_axis=0, concat_axis=0, tiled=True
    )
    sent = flight.step(token, "small")
    sent = flight.step(sent[0], "a", "b", joint=True)
    token = after(sent[0], sent[1])
    sent = flight.step(token, "small")
    sent = flight.step(sent[0], "small")
    flight.finish(sent[0], "a")
    ready = flight.done["a"]
    ready = (after(ready[0], *sent),) + ready[1:]
    weights = unpack_grads(core_side, ready, width, ff, spans["a"][0])
    sent = flight.step(weights[0], "small")
    grad_ocean_state = from_channel_rows(after(received, *sent), half, dates, cols, group_ch)
    sent = flight.step(grad_ocean_state, "small")
    flight.finish(sent[0], "b")
    weights = (after(weights[0], *sent), weights[1])
    weights = unpack_grads(core_side, flight.done["b"], width, ff, spans["b"][0], weights)
    flight.finish(weights[0], "small")
    g_out_slots, g_in_slots, g_w_depth, g_b_in = unpack(in_order(*flight.done["small"]), last_sums)
    grad_w_one, grad_w_two = weights
    grad_w_out = jnp.einsum("sd,sc->dc", g_out_slots.astype(F32), table, precision=exact_mode)
    count = -(-ff // width)
    grad_b_one = summed[2 : 2 + count].reshape(-1)[:ff]
    grad_b_two = summed[2 + count]
    grad_b_out = jnp.dot(summed[3 + count, :slots], table, precision=exact_mode)
    grad_w_in = jnp.dot(table.T, g_in_slots.astype(F32), precision=exact_mode)
    grad_w_depth = g_w_depth.astype(F32).reshape(kernel, kernel, width)
    grad_b_in = g_b_in.astype(F32).reshape(-1)
    return (
        next_state,
        grad_ocean_state,
        grad_w_in,
        grad_b_in,
        grad_w_depth,
        norm_grads[1],
        norm_grads[0],
        grad_w_one,
        grad_b_one,
        grad_w_two.T,
        grad_b_two,
        grad_w_out,
        grad_b_out,
    )


def solution(mesh):
    return jax.shard_map(
        on_device,
        mesh=mesh,
        in_specs=(
            P(None, None, "sp", "lev"),
            P(),
            P("lev", "sp"),
            P(),
            P(),
            P(),
            P(),
            P(),
            P(),
            P(),
            P(),
            P(),
            P(),
            P(),
            P(None, None, "sp", "lev"),
        ),
        out_specs=(
            P(None, None, "sp", "lev"),
            P(None, None, "sp", "lev"),
            P(),
            P(),
            P(),
            P(),
            P(),
            P(),
            P(),
            P(),
            P(),
            P(),
            P(),
        ),
        check_vma=False,
    )
```

```python
import functools

import jax
import jax.numpy as jnp
from jax import lax
from jax.experimental import pallas as pl
from jax.experimental.pallas import tpu as pltpu
from jax.sharding import PartitionSpec as P

VARS = 10
LANES = 128
SUBLANES = 8

exact_mode = lax.Precision.HIGHEST
F32 = jnp.float32
BF16 = jnp.bfloat16

COST = pl.CostEstimate(flops=50000000000, transcendentals=0, bytes_accessed=50000000)

TAIL_SCALE = 0.3
TAIL_POLY = (
    0.119623263,
    0.120845528,
    0.0993471402,
    0.130416391,
    -0.0571672287,
    0.210118226,
    -0.159378204,
    0.0361948279,
)


def slot_table(levels_of_slots, groups, group_ch, padded_ch, channels):
    slot_count = groups * group_ch
    kinds = jnp.arange(slot_count) % VARS
    target = jnp.repeat(levels_of_slots, VARS) * VARS + kinds
    target = jnp.pad(
        target.reshape(groups, group_ch), ((0, 0), (0, padded_ch - group_ch)), constant_values=-1
    ).reshape(-1)
    columns = jnp.arange(channels)
    return (target[:, None] == columns[None, :]).astype(F32)


def bits_of(axis):
    size = lax.axis_size(axis)
    return [(axis, 1 << k) for k in range(size.bit_length() - 1)]


def hop(value, stage):
    axis, bit = stage
    return lax.ppermute(value, axis, [(i, i ^ bit) for i in range(lax.axis_size(axis))])


def side(stage):
    axis, bit = stage
    return (lax.axis_index(axis) // bit) % 2


def butterfly(value, stages):
    for stage in stages:
        value = value + hop(value, stage)
    return value


def after(value, *earlier):
    return lax.optimization_barrier((value,) + earlier)[0]


def halves(value, axis, bit):
    half = value.shape[axis] // 2
    stay = lax.dynamic_slice_in_dim(value, bit * half, half, axis)
    sent = lax.dynamic_slice_in_dim(value, (1 - bit) * half, half, axis)
    return stay, sent


def halving_lanes(lanes):
    tiles = lanes // LANES
    return lanes % LANES == 0 and (tiles % 2 == 0 or tiles >= 9)


def total(terms):
    value = terms[0].astype(F32)
    for term in terms[1:]:
        value = value + term.astype(F32)
    return value


def exchange(value, stages, link, partner=None, most=2):
    kept = []
    own = 0
    lanes = value.shape[2]
    terms = [value]
    rest = stages
    if partner is not None:
        terms.append((yield partner, hop(partner, stages[0])))
        rest = stages[1:]
    row_halvings = 0
    for stage in rest:
        bit = side(stage)
        shape = terms[0].shape
        if stage is rest[-1]:
            axis = None
        elif shape[0] % 2 == 0 and row_halvings < most:
            axis = 0
            row_halvings += 1
            own = own * 2 + bit
        else:
            axis = 2 if halving_lanes(shape[2]) else None
        if axis is None:
            sent = total(terms).astype(link)
            terms = [sent]
        else:
            if axis == 2 and shape[2] // LANES % 2:
                terms = [jnp.pad(term, ((0, 0), (0, 0), (0, LANES))) for term in terms]
            pairs = [halves(term, axis, bit) for term in terms]
            sent = total([pair[1] for pair in pairs]).astype(link)
            terms = [pair[0] for pair in pairs]
            kept.append((stage, axis))
        terms.append((yield sent, hop(sent, stage)))
    value = total(terms).astype(link)
    for stage, axis in reversed(kept):
        came = yield value, hop(value, stage)
        if axis == 0:
            value = jnp.concatenate([value, came], axis=0)
        else:
            bit = side(stage)
            low = jnp.where(bit == 0, value, came)
            high = jnp.where(bit == 0, came, value)
            value = jnp.concatenate([low, high], axis=2)[:, :, :lanes]
    other = None
    if partner is not None:
        other = yield value, hop(value, stages[0])
    yield value, other, own, 1 << row_halvings


def in_order(value, other, own, pieces):
    count = value.shape[0] // pieces
    return jnp.concatenate(
        [lax.dynamic_slice_in_dim(value, (index ^ own) * count, count, 0) for index in range(pieces)],
        axis=0,
    )


class Exchanges:
    def __init__(self):
        self.running = {}
        self.came = {}
        self.done = {}

    def hold(self, name, got):
        if len(got) == 2:
            self.came[name] = got[1]
            return [got[0]]
        self.done[name] = got
        del self.running[name]
        return []

    def begin(self, name, *args, **options):
        self.running[name] = exchange(*args, **options)
        return self.hold(name, next(self.running[name]))[0]

    def step(self, token, *names, joint=False):
        names = [name for name in names if name in self.running]
        if joint:
            came = lax.optimization_barrier(tuple(self.came[name] for name in names) + (token,))
        else:
            came = [after(self.came[name], token) for name in names]
        sent = []
        for name, value in zip(names, came):
            sent += self.hold(name, self.running[name].send(value))
        return sent

    def finish(self, token, *names):
        while any(name in self.running for name in names):
            self.step(token, *names)


def unpack_grads(core_side, reduced, width, ff, start, prior=()):
    value, other, own, pieces = reduced
    count = value.shape[0] // pieces
    rows = count * SUBLANES
    columns = value.shape[2]

    def body(own_ref, value_ref, other_ref, *refs):
        out_one, out_two = refs[len(prior) :]
        mine = value_ref[...].astype(F32).reshape(rows, columns)
        theirs = other_ref[...].astype(F32).reshape(rows, columns)
        first = own_ref[1] == 0

        @pl.when(first)
        def _():
            out_one[...] = mine
            out_two[...] = theirs

        @pl.when(jnp.logical_not(first))
        def _():
            out_one[...] = theirs
            out_two[...] = mine

    out = pl.BlockSpec((pl.Element(rows), pl.Element(columns)), lambda i, own: (i * rows, start))
    piece = pl.BlockSpec((count, SUBLANES, columns), lambda i, own: (i ^ own[0], 0, 0))
    return pl.pallas_call(
        body,
        grid_spec=pltpu.PrefetchScalarGridSpec(
            num_scalar_prefetch=1,
            grid=(pieces,),
            in_specs=[piece, piece] + [pl.BlockSpec(memory_space=pl.ANY)] * len(prior),
            out_specs=[out, out],
        ),
        out_shape=[jax.ShapeDtypeStruct((width, ff), F32)] * 2,
        input_output_aliases={3 + k: k for k in range(len(prior))},
        cost_estimate=COST,
        name="unpack_grads",
    )(jnp.stack([own, core_side]).astype(jnp.int32), value, other, *prior)


def pixel_order(dates, cols):
    pixels = dates * cols
    source = lax.broadcasted_iota(jnp.int32, (pixels, pixels), 0)
    place = lax.broadcasted_iota(jnp.int32, (pixels, pixels), 1)
    return ((source % cols) * dates + source // cols == place).astype(BF16)


def to_channel_rows(state, cotangent, groups, half, padded_ch):
    all_rows, dates, cols, ch = state.shape
    rows = all_rows // groups
    high = rows + 2 * half
    pixels = dates * cols

    def body(state_ref, cot_ref, window_ref, ct_ref):
        perm = pixel_order(dates, cols)
        blank = jnp.zeros((padded_ch - ch, pixels), F32)
        zero = jnp.zeros((padded_ch, pixels), BF16)

        def turned(ref, row):
            value = lax.dot_general(
                ref[row].reshape(pixels, ch), perm, (((0,), (0,)), ((), ())), preferred_element_type=F32
            )
            return jnp.concatenate([value, blank], axis=0).astype(BF16) if padded_ch > ch else value.astype(BF16)

        for row in range(half):
            window_ref[0, row] = zero
            window_ref[groups - 1, half + rows + row] = zero
        for row in range(all_rows):
            value = turned(state_ref, row)
            for band in range(groups):
                place = row - band * rows + half
                if 0 <= place < high:
                    window_ref[band, place] = value
            ct_ref[row // rows, row % rows] = turned(cot_ref, row)

    return pl.pallas_call(
        body,
        out_shape=[
            jax.ShapeDtypeStruct((groups, high, padded_ch, pixels), BF16),
            jax.ShapeDtypeStruct((groups, rows, padded_ch, pixels), BF16),
        ],
        cost_estimate=COST,
        name="to_channel_rows",
    )(state, cotangent)


def from_channel_rows(windows, half, dates, cols, ch):
    groups, high, padded_ch, pixels = windows.shape
    rows = high - 2 * half

    def body(window_ref, out_ref):
        perm = pixel_order(dates, cols)
        for row in range(groups * rows):
            value = None
            for band in range(groups):
                place = row - band * rows + half
                if 0 <= place < high:
                    piece = window_ref[band, place]
                    value = piece if value is None else value.astype(F32) + piece.astype(F32)
            value = lax.dot_general(
                perm, value.astype(BF16), (((1,), (1,)), ((), ())), preferred_element_type=F32
            )
            out_ref[row] = value[:, :ch].astype(BF16).reshape(dates, cols, ch)

    return pl.pallas_call(
        body,
        out_shape=jax.ShapeDtypeStruct((groups * rows, dates, cols, ch), BF16),
        cost_estimate=COST,
        name="from_channel_rows",
    )(windows)


def to_pixel_rows(received):
    groups, rows, padded_ch, pixels = received.shape
    slots = groups * padded_ch

    def body(in_ref, out_ref):
        for row in range(rows):
            value = jnp.concatenate([in_ref[g, row].astype(F32) for g in range(groups)], axis=0)
            out_ref[row] = value.T.astype(BF16)

    return pl.pallas_call(
        body,
        out_shape=jax.ShapeDtypeStruct((rows, pixels, slots), BF16),
        cost_estimate=COST,
        name="to_pixel_rows",
    )(received)


def hidden_conv_body(rows, cols, half, edge_ref, x_ref, low_x_ref, high_x_ref, w_ref, b_ref, depth_ref, hidden_ref, low_ref, conv_ref, stat_ref, pad_ref):
    kernel = 2 * half + 1
    high = rows + 2 * half

    def hidden_of(ref, columns):
        value = jnp.dot(ref[...], w_ref[...], preferred_element_type=F32) + b_ref[...]
        return value.reshape(high, columns, SUBLANES, LANES)

    value = hidden_of(x_ref, cols)
    hidden_ref[...] = value[half : half + rows]
    pad_ref[:, half : half + cols] = value.astype(BF16).astype(F32)
    pad_ref[:, :half] = hidden_of(low_x_ref, half).astype(BF16).astype(F32)
    pad_ref[:, half + cols :] = hidden_of(high_x_ref, half).astype(BF16).astype(F32)

    @pl.when(edge_ref[0] == 1)
    def _():
        pad_ref[:half] = jnp.zeros((half,) + pad_ref.shape[1:], F32)

    @pl.when(edge_ref[1] == 1)
    def _():
        pad_ref[half + rows :] = jnp.zeros((half,) + pad_ref.shape[1:], F32)

    @pl.when(edge_ref[2] == 1)
    def _():
        pad_ref[:, :half] = jnp.zeros((pad_ref.shape[0], half) + pad_ref.shape[2:], F32)

    @pl.when(edge_ref[3] == 1)
    def _():
        pad_ref[:, half + cols :] = jnp.zeros((pad_ref.shape[0], half) + pad_ref.shape[2:], F32)

    low_ref[...] = pad_ref[...].reshape(low_ref.shape).astype(BF16)

    def one_row(row, carry):
        total, square = carry
        acc = jnp.zeros((cols, SUBLANES, LANES), F32)
        for i in range(kernel):
            slab = pad_ref[row + i]
            for j in range(kernel):
                acc = acc + slab[j : j + cols] * depth_ref[i * kernel + j]
        conv_ref[row] = acc
        return total + jnp.sum(acc, axis=0), square + jnp.sum(acc * acc, axis=0)

    zero = jnp.zeros((SUBLANES, LANES), F32)
    total, square = lax.fori_loop(0, rows, one_row, (zero, zero))
    stat_ref[0:1] = jnp.sum(total, axis=0, keepdims=True)
    stat_ref[1:2] = jnp.sum(square, axis=0, keepdims=True)


def hidden_conv(edges, x, low_x, high_x, w_slots, b_in, depth, tile):
    rows, cols, dates, half = tile
    slots, width = w_slots.shape
    padded = (rows + 2 * half) * (cols + 2 * half) * dates
    return pl.pallas_call(
        functools.partial(hidden_conv_body, rows, cols, half),
        grid=(pl.cdiv(width, LANES),),
        in_specs=[
            pl.BlockSpec(memory_space=pltpu.SMEM),
            pl.BlockSpec(x.shape, lambda i: (0, 0)),
            pl.BlockSpec(low_x.shape, lambda i: (0, 0)),
            pl.BlockSpec(high_x.shape, lambda i: (0, 0)),
            pl.BlockSpec((slots, LANES), lambda i: (0, i)),
            pl.BlockSpec((1, LANES), lambda i: (0, i)),
            pl.BlockSpec((depth.shape[0], 1, LANES), lambda i: (0, 0, i)),
        ],
        out_specs=[
            pl.BlockSpec((rows, cols, dates, LANES), lambda i: (0, 0, 0, i)),
            pl.BlockSpec((padded, LANES), lambda i: (0, i)),
            pl.BlockSpec((rows, cols, dates, LANES), lambda i: (0, 0, 0, i)),
            pl.BlockSpec((2, LANES), lambda i: (0, i)),
        ],
        out_shape=[
            jax.ShapeDtypeStruct((rows, cols, dates, width), F32),
            jax.ShapeDtypeStruct((padded, width), BF16),
            jax.ShapeDtypeStruct((rows, cols, dates, width), F32),
            jax.ShapeDtypeStruct((2, width), F32),
        ],
        scratch_shapes=[pltpu.VMEM((rows + 2 * half, cols + 2 * half, dates, LANES), F32)],

        cost_estimate=COST,
        name="hidden_conv",
    )(edges, x, low_x, high_x, w_slots, b_in.reshape(1, -1), depth)


def gelu_pair(values):
    size = jnp.abs(values)
    gauss = jnp.exp(-0.5 * values * values)
    t = 1.0 / (1.0 + TAIL_SCALE * size)
    poly = jnp.full_like(t, TAIL_POLY[-1])
    for factor in TAIL_POLY[-2::-1]:
        poly = poly * t + factor
    tail = gauss * (t * poly)
    below = jnp.where(values >= 0, 1.0 - tail, tail)
    return values * below, below + values * (gauss * 0.3989422804014327)


def mlp_body(row_block, core_ref, conv_ref, norm_ref, branch_ref, w_one_ref, b_one_ref, w_two_ref, act_ref, dup_ref, keep_ref, send_ref, gb_ref, normed_ref, normed_t, branch_t):
    @pl.when(pl.program_id(0) == 0)
    def _():
        centered = (conv_ref[...] - norm_ref[0:1]) * norm_ref[1:2]
        normed_ref[...] = (centered * norm_ref[2:3] + norm_ref[3:4]).astype(BF16)
        normed_t[...] = normed_ref[...].T
        branch_t[...] = branch_ref[...].T

    total = jnp.zeros((1, act_ref.shape[1]), F32)
    for start in range(0, normed_ref.shape[0], row_block):
        rows = pl.ds(start, row_block)
        up = jnp.dot(normed_ref[rows], w_one_ref[...], preferred_element_type=F32) + b_one_ref[...]
        d_act = jnp.dot(branch_ref[rows], w_two_ref[...], preferred_element_type=F32)
        value, slope = gelu_pair(up)
        act_ref[rows] = value.astype(BF16)
        d_up = (slope * d_act).astype(BF16)
        dup_ref[rows] = d_up
        total = total + jnp.sum(d_up.astype(F32), axis=0, keepdims=True)
    gb_ref[...] = total
    grad_one = jnp.dot(normed_t[...], dup_ref[...], preferred_element_type=F32).astype(BF16)
    grad_two = jnp.dot(branch_t[...], act_ref[...], preferred_element_type=F32).astype(BF16)
    first = core_ref[0] == 0

    @pl.when(first)
    def _():
        keep_ref[...] = grad_one
        send_ref[...] = grad_two

    @pl.when(jnp.logical_not(first))
    def _():
        keep_ref[...] = grad_two
        send_ref[...] = grad_one


def mlp(core_side, conv_flat, norm, d_branch, w_one, b_one, w_two, first, last, prior=(), block=256, row_block=128):
    pixels, width = conv_flat.shape
    hidden = w_one.shape[1]
    start = first // block

    def body(core_ref, conv_ref, norm_ref, branch_ref, w_one_ref, b_one_ref, w_two_ref, *refs):
        mlp_body(row_block, core_ref, conv_ref, norm_ref, branch_ref, w_one_ref, b_one_ref, w_two_ref, *refs[len(prior) :])

    whole = jax.ShapeDtypeStruct((pixels, hidden), BF16)
    grad = jax.ShapeDtypeStruct((width, last - first), BF16)
    results = pl.pallas_call(
        body,
        grid=(pl.cdiv(last - first, block),),
        in_specs=[
            pl.BlockSpec(memory_space=pltpu.SMEM),
            pl.BlockSpec((pixels, width), lambda i: (0, 0)),
            pl.BlockSpec((4, width), lambda i: (0, 0)),
            pl.BlockSpec((pixels, width), lambda i: (0, 0)),
            pl.BlockSpec((width, block), lambda i: (0, start + i)),
            pl.BlockSpec((1, block), lambda i: (0, start + i)),
            pl.BlockSpec((width, block), lambda i: (0, start + i)),
        ]
        + [pl.BlockSpec(memory_space=pl.ANY)] * len(prior),
        out_specs=[
            pl.BlockSpec((pixels, block), lambda i: (0, start + i)),
            pl.BlockSpec((pixels, block), lambda i: (0, start + i)),
            pl.BlockSpec((width, block), lambda i: (0, i)),
            pl.BlockSpec((width, block), lambda i: (0, i)),
            pl.BlockSpec((1, block), lambda i: (0, start + i)),
        ],
        out_shape=[whole, whole, grad, grad, jax.ShapeDtypeStruct((1, hidden), F32)],
        scratch_shapes=[pltpu.VMEM((pixels, width), BF16)] + [pltpu.VMEM((width, pixels), BF16)] * 2,
        input_output_aliases={7 + n: k for n, k in enumerate((0, 1, 4)[: len(prior)])},

        cost_estimate=COST,
        name="mlp",
    )(core_side.reshape(1).astype(jnp.int32), conv_flat, norm, d_branch, w_one, b_one.reshape(1, -1), w_two, *prior)
    activated, d_up, keep, send, bias = results
    blocks = (width // SUBLANES, SUBLANES, last - first)
    return (activated, d_up, bias), (keep.reshape(blocks), send.reshape(blocks))


def norm_back_body(dup_ref, w_ref, conv_ref, norm_ref, dn_ref, part_ref):
    value = lax.dot_general(
        dup_ref[...], w_ref[...], (((1,), (1,)), ((), ())), preferred_element_type=F32
    )
    dn_ref[...] = value
    centered = (conv_ref[...] - norm_ref[0:1]) * norm_ref[1:2]

    @pl.when(pl.program_id(0) == 0)
    def _():
        part_ref[...] = jnp.zeros(part_ref.shape, F32)

    part_ref[0:1] += jnp.sum(value, axis=0, keepdims=True)
    part_ref[1:2] += jnp.sum(value * centered, axis=0, keepdims=True)


def norm_back(d_up, w_one, conv_flat, norm, row_block=256):
    pixels, hidden = d_up.shape
    width = w_one.shape[0]
    return pl.pallas_call(
        norm_back_body,
        grid=(pixels // row_block,),
        in_specs=[
            pl.BlockSpec((row_block, hidden), lambda i: (i, 0)),
            pl.BlockSpec((width, hidden), lambda i: (0, 0)),
            pl.BlockSpec((row_block, width), lambda i: (i, 0)),
            pl.BlockSpec((4, width), lambda i: (0, 0)),
        ],
        out_specs=[
            pl.BlockSpec((row_block, width), lambda i: (i, 0)),
            pl.BlockSpec((2, width), lambda i: (0, 0)),
        ],
        out_shape=[
            jax.ShapeDtypeStruct((pixels, width), F32),
            jax.ShapeDtypeStruct((2, width), F32),
        ],

        cost_estimate=COST,
        name="norm_back",
    )(d_up, w_one, conv_flat, norm)


def branch_out_body(act_ref, w_ref, b_ref, hidden_ref, wet_ref, w_out_ref, b_out_ref, dres_ref, result_ref, gout_ref):
    branch = b_ref[...] + lax.dot_general(
        act_ref[...], w_ref[...], (((1,), (1,)), ((), ())), preferred_element_type=F32
    )
    mixed = ((hidden_ref[...] + branch) * wet_ref[...]).astype(BF16)
    result = jnp.dot(mixed, w_out_ref[...], preferred_element_type=F32) + b_out_ref[...]
    result = result.T
    groups, count, padded_ch, lanes = result_ref.shape
    for row in range(count):
        for g in range(groups):
            piece = result[g * padded_ch : (g + 1) * padded_ch, row * lanes : (row + 1) * lanes]
            result_ref[g, row] = piece.astype(BF16)

    @pl.when(pl.program_id(0) == 0)
    def _():
        gout_ref[...] = jnp.zeros(gout_ref.shape, F32)

    gout_ref[...] += lax.dot_general(
        dres_ref[...], mixed, (((0,), (0,)), ((), ())), preferred_element_type=F32
    )


def branch_out(activated, w_two, b_two, hidden, wet, w_out_slots, b_slots, d_result, out_shape, row_block=256):
    pixels, inner = activated.shape
    width, slots = w_out_slots.shape
    return pl.pallas_call(
        branch_out_body,
        grid=(pixels // row_block,),
        in_specs=[
            pl.BlockSpec((row_block, inner), lambda i: (i, 0)),
            pl.BlockSpec((width, inner), lambda i: (0, 0)),
            pl.BlockSpec((1, width), lambda i: (0, 0)),
            pl.BlockSpec((row_block, width), lambda i: (i, 0)),
            pl.BlockSpec((row_block, 1), lambda i: (i, 0)),
            pl.BlockSpec((width, slots), lambda i: (0, 0)),
            pl.BlockSpec((1, slots), lambda i: (0, 0)),
            pl.BlockSpec((row_block, slots), lambda i: (i, 0)),
        ],
        out_specs=[
            pl.BlockSpec(
                (out_shape[0], row_block // out_shape[3]) + out_shape[2:], lambda i: (0, i, 0, 0)
            ),
            pl.BlockSpec((slots, width), lambda i: (0, 0)),
        ],
        out_shape=[
            jax.ShapeDtypeStruct(out_shape, BF16),
            jax.ShapeDtypeStruct((slots, width), F32),
        ],

        cost_estimate=COST,
        name="branch_out",
    )(activated, w_two, b_two.reshape(1, -1), hidden, wet, w_out_slots, b_slots.reshape(1, -1), d_result)


def conv_back_body(rows, cols, half, edge_ref, coef_ref, dn_ref, conv_ref, dsum_ref, low_ref, depth_ref, dh_ref, dh_low_ref, dh_high_ref, gw_ref, gb_ref, dc_ref, dl_ref, pad_ref, tap_ref):
    kernel = 2 * half + 1
    wide = cols + 2 * half
    d_conv = coef_ref[0:1] * dn_ref[...] + (coef_ref[1:2] * conv_ref[...] + coef_ref[2:3])
    dc_ref[...] = d_conv.astype(BF16).astype(F32)
    dl_ref[...] = jnp.zeros(dl_ref.shape, F32)
    dl_ref[half : half + rows, half : half + cols] = dsum_ref[...]
    pad_ref[...] = low_ref[...].astype(F32).reshape(pad_ref.shape)
    tap_ref[...] = jnp.zeros(tap_ref.shape, F32)

    def one_row(row, carry):
        source = [dc_ref[row, c] for c in range(cols)]
        for i in range(kernel):
            taps = [jnp.broadcast_to(depth_ref[i * kernel + j], (SUBLANES, LANES)) for j in range(kernel)]
            for c in range(wide):
                acc = dl_ref[row + i, c]
                for j in range(kernel):
                    if 0 <= c - j < cols:
                        acc = acc + source[c - j] * taps[j]
                dl_ref[row + i, c] = acc
        for i in range(kernel):
            sums = [tap_ref[i * kernel + j] for j in range(kernel)]
            for c in range(wide):
                value = pad_ref[row + i, c]
                for j in range(kernel):
                    if 0 <= c - j < cols:
                        sums[j] = sums[j] + source[c - j] * value
            for j in range(kernel):
                tap_ref[i * kernel + j] = sums[j]
        return carry

    lax.fori_loop(0, rows, one_row, 0)

    @pl.when(edge_ref[0] == 1)
    def _():
        dl_ref[:half] = jnp.zeros((half,) + dl_ref.shape[1:], F32)

    @pl.when(edge_ref[1] == 1)
    def _():
        dl_ref[half + rows :] = jnp.zeros((half,) + dl_ref.shape[1:], F32)

    @pl.when(edge_ref[2] == 1)
    def _():
        dl_ref[:, :half] = jnp.zeros((dl_ref.shape[0], half) + dl_ref.shape[2:], F32)

    @pl.when(edge_ref[3] == 1)
    def _():
        dl_ref[:, half + cols :] = jnp.zeros((dl_ref.shape[0], half) + dl_ref.shape[2:], F32)

    d_hidden = dl_ref[...]
    dh_ref[...] = d_hidden[:, half : half + cols].reshape(dh_ref.shape).astype(BF16)
    dh_low_ref[...] = d_hidden[:, :half].reshape(dh_low_ref.shape).astype(BF16)
    dh_high_ref[...] = d_hidden[:, half + cols :].reshape(dh_high_ref.shape).astype(BF16)
    gb_ref[...] = jnp.sum(jnp.sum(d_hidden, axis=(0, 1)), axis=0, keepdims=True)
    gw_ref[...] = jnp.sum(tap_ref[...], axis=1)


def conv_back(edges, coef, d_normed, conv_out, d_sum, lowered, depth, tile, first, last, prior=()):
    rows, cols, dates, half = tile
    taps = depth.shape[0]
    width = lowered.shape[1]
    padded = lowered.shape[0]
    inner = pl.BlockSpec((rows, cols, dates, LANES), lambda i: (0, 0, 0, first + i))
    wide = (rows + 2 * half, cols + 2 * half, dates, LANES)
    inside = (rows + 2 * half) * cols * dates
    beside = (rows + 2 * half) * half * dates

    def body(edge_ref, coef_ref, dn_ref, conv_ref, dsum_ref, low_ref, depth_ref, *refs):
        conv_back_body(rows, cols, half, edge_ref, coef_ref, dn_ref, conv_ref, dsum_ref, low_ref, depth_ref, *refs[len(prior) :])

    return pl.pallas_call(
        body,
        grid=(last - first,),
        in_specs=[
            pl.BlockSpec(memory_space=pltpu.SMEM),
            pl.BlockSpec((3, LANES), lambda i: (0, first + i)),
            inner,
            inner,
            inner,
            pl.BlockSpec((padded, LANES), lambda i: (0, first + i)),
            pl.BlockSpec((taps, 1, LANES), lambda i: (0, 0, first + i)),
        ]
        + [pl.BlockSpec(memory_space=pl.ANY)] * len(prior),
        out_specs=[
            pl.BlockSpec((count, LANES), lambda i: (0, first + i)) for count in (inside, beside, beside, taps, 1)
        ],
        out_shape=[
            jax.ShapeDtypeStruct((inside, width), BF16),
            jax.ShapeDtypeStruct((beside, width), BF16),
            jax.ShapeDtypeStruct((beside, width), BF16),
            jax.ShapeDtypeStruct((taps, width), F32),
            jax.ShapeDtypeStruct((1, width), F32),
        ],
        scratch_shapes=[
            pltpu.VMEM((rows, cols, dates, LANES), F32),
            pltpu.VMEM(wide, F32),
            pltpu.VMEM(wide, F32),
            pltpu.VMEM((taps, dates, LANES), F32),
        ],
        input_output_aliases={7 + k: k for k in range(len(prior))},

        cost_estimate=COST,
        name="conv_back",
    )(edges, coef, d_normed, conv_out, d_sum, lowered, depth, *prior)


def input_back(dh, dh_low, dh_high, x, x_low, x_high, w_slots):
    slots, width = w_slots.shape
    inside, beside = dh.shape[0], dh_low.shape[0]
    row_block = inside // 2
    mix = (((1,), (1,)), ((), ()))
    down = (((0,), (0,)), ((), ()))

    def body(dh_ref, dl_ref, dr_ref, x_ref, xl_ref, xr_ref, w_ref, ds_ref, sl_ref, sr_ref, g_ref):
        ds_ref[...] = lax.dot_general(dh_ref[...], w_ref[...], mix, preferred_element_type=F32)

        @pl.when(pl.program_id(0) == 0)
        def _():
            sl_ref[...] = lax.dot_general(
                dl_ref[...], w_ref[...], mix, preferred_element_type=F32
            ).astype(BF16)
            sr_ref[...] = lax.dot_general(
                dr_ref[...], w_ref[...], mix, preferred_element_type=F32
            ).astype(BF16)
            g_ref[...] = lax.dot_general(
                xl_ref[...], dl_ref[...], down, preferred_element_type=F32
            ) + lax.dot_general(xr_ref[...], dr_ref[...], down, preferred_element_type=F32)

        g_ref[...] += lax.dot_general(x_ref[...], dh_ref[...], down, preferred_element_type=F32)

    moving = lambda i: (i, 0)
    fixed = lambda i: (0, 0)
    return pl.pallas_call(
        body,
        grid=(inside // row_block,),
        in_specs=[
            pl.BlockSpec((row_block, width), moving),
            pl.BlockSpec((beside, width), fixed),
            pl.BlockSpec((beside, width), fixed),
            pl.BlockSpec((row_block, slots), moving),
            pl.BlockSpec((beside, slots), fixed),
            pl.BlockSpec((beside, slots), fixed),
            pl.BlockSpec((slots, width), fixed),
        ],
        out_specs=[
            pl.BlockSpec((row_block, slots), moving),
            pl.BlockSpec((beside, slots), fixed),
            pl.BlockSpec((beside, slots), fixed),
            pl.BlockSpec((slots, width), fixed),
        ],
        out_shape=[
            jax.ShapeDtypeStruct((inside, slots), F32),
            jax.ShapeDtypeStruct((beside, slots), BF16),
            jax.ShapeDtypeStruct((beside, slots), BF16),
            jax.ShapeDtypeStruct((slots, width), F32),
        ],
        cost_estimate=COST,
        name="input_back",
    )(dh, dh_low, dh_high, x, x_low, x_high, w_slots)


def to_groups(d_state, from_high, from_low, groups):
    rows, pixels, slots = d_state.shape
    beside = from_low.shape[1]
    padded_ch = slots // groups

    def body(in_ref, high_ref, low_ref, out_ref):
        for row in range(rows):
            value = in_ref[row]
            first = value[:beside] + low_ref[row].astype(F32)
            last = value[pixels - beside :] + high_ref[row].astype(F32)
            value = jnp.concatenate([first, value[beside : pixels - beside], last], axis=0).T
            for g in range(groups):
                out_ref[g, row] = value[g * padded_ch : (g + 1) * padded_ch].astype(BF16)

    return pl.pallas_call(
        body,
        out_shape=jax.ShapeDtypeStruct((groups, rows, padded_ch, pixels), BF16),
        cost_estimate=COST,
        name="to_groups",
    )(d_state, from_high, from_low)


def on_device(
    ocean_state,
    slot_level,
    wet_mask,
    w_in,
    b_in,
    w_depth,
    norm_gain,
    norm_bias,
    w_one,
    b_one,
    w_two,
    b_two,
    w_out,
    b_out,
    cotangent,
):
    groups = lax.axis_size("lev")
    strips = lax.axis_size("sp")
    group_index = lax.axis_index("lev")
    strip_index = lax.axis_index("sp")
    rows, cols = wet_mask.shape
    all_rows, dates, _, group_ch = ocean_state.shape
    padded_ch = -(-group_ch // SUBLANES) * SUBLANES
    slots = padded_ch * groups
    channels, width = w_in.shape
    kernel = w_depth.shape[0]
    half = kernel // 2
    tile = (rows, cols, dates, half)
    high_rows = rows + 2 * half
    pixels = rows * cols * dates
    pixel_total = float(pixels * groups * strips)

    lev_stages = bits_of("lev")
    sp_stages = bits_of("sp")
    stages = lev_stages + sp_stages
    core, lev_rest = lev_stages[:1], lev_stages[1:]
    orders = (
        core + lev_rest + sp_stages,
        core + sp_stages[:1] + lev_rest + sp_stages[1:],
        core + sp_stages[1:2] + lev_rest + sp_stages[:1] + sp_stages[2:],
        core + sp_stages[1:] + sp_stages[:1] + lev_rest,
    )
    forward = [(i, i + 1) for i in range(strips - 1)]
    backward = [(i + 1, i) for i in range(strips - 1)]
    edges = jnp.stack(
        [group_index == 0, group_index == groups - 1, strip_index == 0, strip_index == strips - 1]
    ).astype(jnp.int32)

    table = slot_table(slot_level, groups, group_ch, padded_ch, channels)
    table_low = table.astype(BF16)
    w_slots = jnp.dot(table_low, w_in, preferred_element_type=F32).astype(BF16)
    w_out_slots = jnp.dot(w_out, table_low.T, preferred_element_type=F32).astype(BF16)
    b_slots = jnp.dot(table, b_out, precision=exact_mode)
    depth = w_depth.astype(F32).reshape(kernel * kernel, 1, width)

    row_pixels = cols * dates
    beside = half * dates
    windows, d_result = to_channel_rows(ocean_state, cotangent, groups, half, padded_ch)
    windows = lax.all_to_all(windows, "lev", split_axis=0, concat_axis=0, tiled=True)
    d_result = lax.all_to_all(
        after(d_result, windows), "lev", split_axis=0, concat_axis=0, tiled=True
    )
    x_rows = to_pixel_rows(windows)
    x_low = lax.ppermute(x_rows[:, row_pixels - beside :], "sp", forward).reshape(-1, slots)
    x_high = lax.ppermute(x_rows[:, :beside], "sp", backward).reshape(-1, slots)
    x_rows = x_rows.reshape(-1, slots)
    d_result = to_pixel_rows(d_result).reshape(pixels, slots)

    hidden, lowered, conv_out, local = hidden_conv(
        edges, x_rows, x_low, x_high, w_slots, b_in, depth, tile
    )
    came = hop(local, stages[0])
    wet = jnp.broadcast_to(
        wet_mask.astype(F32)[:, :, None, None], (rows, cols, dates, 1)
    ).reshape(pixels, 1)
    d_mixed = jnp.dot(d_result, w_out_slots.T, preferred_element_type=F32)
    d_sum = d_mixed * wet
    d_branch = d_sum.astype(BF16)
    g_b_two = jnp.sum(d_branch.astype(F32), axis=0)
    g_bias_slots = jnp.sum(d_result.astype(F32), axis=0)

    sums = butterfly(local + after(came, d_branch), stages[1:])
    mean_value = sums[0] / pixel_total
    inv_scale = lax.rsqrt(sums[1] / pixel_total - mean_value * mean_value + 1e-05)
    conv_flat = conv_out.reshape(pixels, width)
    norm = jnp.stack([mean_value, inv_scale, norm_gain, norm_bias])
    ff = w_one.shape[1]
    block = 256
    cut = ff // 2 // block * block
    spans = {"a": (cut, ff), "b": (0, cut)}
    flight = Exchanges()

    def as_rows(vector):
        flat = vector.reshape(-1)
        count = -(-flat.shape[0] // width)
        return jnp.pad(flat, (0, count * width - flat.shape[0])).reshape(count, width)

    w_two_t = w_two.T
    core_side = side(core[0])

    def part(name, order, prior=()):
        found, grads = mlp(
            core_side, conv_flat, norm, d_branch, w_one, b_one, w_two_t, *spans[name], prior
        )
        return found, flight.begin(name, grads[0], order, BF16, partner=grads[1])

    found, sent = part("a", orders[0])
    found, sent = part("b", orders[1], (after(found[0], sent),) + found[1:])
    activated, d_up, g_b_one = found
    sent = [sent] + flight.step(g_b_one, "a")

    d_normed, parts = norm_back(after(d_up, *sent), w_one, conv_flat, norm)
    sent = flight.step(parts, "b")
    parts = jnp.concatenate(
        [parts, as_rows(g_b_one), as_rows(g_b_two), as_rows(g_bias_slots)], axis=0
    )
    first_hop = hop(parts, stages[0])
    result, g_out_slots = branch_out(
        after(activated, *sent),
        w_two_t,
        b_two,
        hidden.reshape(pixels, width),
        wet,
        w_out_slots,
        b_slots,
        d_result,
        (groups, rows, padded_ch, row_pixels),
    )
    sent = flight.step(g_out_slots, "a")
    result = after(result, *sent)
    next_state = lax.all_to_all(result, "lev", split_axis=0, concat_axis=0, tiled=True)
    first_hop = after(first_hop, g_out_slots, *sent)
    summed = butterfly(parts + first_hop, stages[1:])
    norm_grads = summed[:2]
    sent = flight.step(summed, "b")

    scale = norm_gain * inv_scale
    slope = scale * inv_scale * (norm_grads[1] / pixel_total)
    coef = jnp.stack(
        [scale, -slope, slope * mean_value - scale * (norm_grads[0] / pixel_total)]
    )
    shape4 = (rows, cols, dates, width)
    inputs = (d_normed.reshape(shape4), conv_out, d_sum.reshape(shape4), lowered, depth, tile)
    tiles = pl.cdiv(width, LANES)
    steps = [0, tiles - 4, tiles - 2, tiles]
    found = ()
    for number, (first, last) in enumerate(zip(steps[:-1], steps[1:])):
        found = conv_back(edges, after(coef, *sent), *inputs, first, last, found)
        if number < 2:
            sent = flight.step(found[4], "b", "a")
    d_hidden, d_low, d_high, g_w_depth, g_b_in = found

    d_state, d_low, d_high, g_in_slots = input_back(
        d_hidden, d_low, d_high, x_rows, x_low, x_high, w_slots
    )
    from_high = lax.ppermute(d_low.reshape(high_rows, beside, slots), "sp", backward)
    from_low = lax.ppermute(d_high.reshape(high_rows, beside, slots), "sp", forward)

    def pack(arrays):
        packed = jnp.concatenate(arrays, axis=0)
        return jnp.pad(packed, ((0, -packed.shape[0] % (16 * SUBLANES)), (0, 0))).reshape(
            -1, SUBLANES, width
        )

    def unpack(packed, arrays):
        packed = packed.reshape(-1, width)
        found = []
        start = 0
        for array in arrays:
            found.append(packed[start : start + array.shape[0]])
            start += array.shape[0]
        return found

    last_sums = [g_out_slots, g_in_slots, g_w_depth, g_b_in]
    sent = [flight.begin("small", pack(last_sums), orders[3], BF16, most=3)]
    sent += flight.step(g_in_slots, "b", "a")
    d_state = to_groups(
        after(d_state, *sent).reshape(high_rows, row_pixels, slots), from_high, from_low, groups
    )
    sent = flight.step(d_state, "small")
    sent = flight.step(sent[0], "b", "a", joint=True)
    next_state = from_channel_rows(after(next_state, *sent), 0, dates, cols, group_ch)
    sent = flight.step(next_state, "small")
    sent = flight.step(sent[0], "b", "a", joint=True)
    token = after(sent[0], sent[1])
    received = lax.all_to_all(
        after(d_state, token), "lev", split_axis=0, concat_axis=0, tiled=True
    )
    sent = flight.step(token, "small")
    sent = flight.step(sent[0], "a", "b", joint=True)
    token = after(sent[0], sent[1])
    sent = flight.step(token, "small")
    sent = flight.step(sent[0], "small")
    flight.finish(sent[0], "a")
    ready = flight.done["a"]
    ready = (after(ready[0], *sent),) + ready[1:]
    weights = unpack_grads(core_side, ready, width, ff, spans["a"][0])
    sent = flight.step(weights[0], "small")
    grad_ocean_state = from_channel_rows(after(received, *sent), half, dates, cols, group_ch)
    sent = flight.step(grad_ocean_state, "small")
    flight.finish(sent[0], "b")
    weights = (after(weights[0], *sent), weights[1])
    weights = unpack_grads(core_side, flight.done["b"], width, ff, spans["b"][0], weights)
    flight.finish(weights[0], "small")
    g_out_slots, g_in_slots, g_w_depth, g_b_in = unpack(in_order(*flight.done["small"]), last_sums)
    grad_w_one, grad_w_two = weights
    grad_w_out = jnp.einsum("sd,sc->dc", g_out_slots.astype(F32), table, precision=exact_mode)
    count = -(-ff // width)
    grad_b_one = summed[2 : 2 + count].reshape(-1)[:ff]
    grad_b_two = summed[2 + count]
    grad_b_out = jnp.dot(summed[3 + count, :slots], table, precision=exact_mode)
    grad_w_in = jnp.dot(table.T, g_in_slots.astype(F32), precision=exact_mode)
    grad_w_depth = g_w_depth.astype(F32).reshape(kernel, kernel, width)
    grad_b_in = g_b_in.astype(F32).reshape(-1)
    return (
        next_state,
        grad_ocean_state,
        grad_w_in,
        grad_b_in,
        grad_w_depth,
        norm_grads[1],
        norm_grads[0],
        grad_w_one,
        grad_b_one,
        grad_w_two.T,
        grad_b_two,
        grad_w_out,
        grad_b_out,
    )


def solution(mesh):
    return jax.shard_map(
        on_device,
        mesh=mesh,
        in_specs=(
            P(None, None, "sp", "lev"),
            P(),
            P("lev", "sp"),
            P(),
            P(),
            P(),
            P(),
            P(),
            P(),
            P(),
            P(),
            P(),
            P(),
            P(),
            P(None, None, "sp", "lev"),
        ),
        out_specs=(
            P(None, None, "sp", "lev"),
            P(None, None, "sp", "lev"),
            P(),
            P(),
            P(),
            P(),
            P(),
            P(),
            P(),
            P(),
            P(),
            P(),
            P(),
        ),
        check_vma=False,
    )
```
